512 devices in a mesh: tok: 16 (over y, x), hid: 32 (over z, core).
Axes of the slice: x: 4, y: 4, z: 16, core: 2. Of those that a mesh axis runs over, the one named last changes fastest.
Arguments:
- tokens: bfloat16 [2048, 8192], P('tok', 'hid'), may hold values from -6 to 6
- gate_weight: bfloat16 [8192, 16384], P('tok', 'hid'), may hold values from -0.09375 to 0.09375
- up_weight: bfloat16 [8192, 16384], P('tok', 'hid'), may hold values from -0.09375 to 0.09375
- down_weight: bfloat16 [16384, 8192], P('hid', 'tok'), may hold values from -0.0625 to 0.0625
- gate_keep: int32 [64, 128], P('tok', 'hid'), may hold values from 0 to 1, as said below
- up_keep: int32 [64, 128], P('tok', 'hid'), may hold values from 0 to 1, as said below
- down_keep: int32 [128, 64], P('hid', 'tok'), may hold values from 0 to 1, as said below
Outputs:
- mixed: bfloat16 [2048, 8192], P('hid', 'tok')
The draws below stay inside these ranges and needn't reach their ends.
Inputs may be any that keep to these rules, and one draw needn't show every extreme that they name: `gate_keep`: in every device's shard of 4 x 4 blocks of a mask, between 4 and 8 blocks are kept; in every mask some shard keeps exactly 8. Shards of down_keep are 4 x 4. `up_keep`: as for gate_keep, drawn independently. `down_keep`: as for gate_keep, drawn independently.
All inputs are finite; a program needn't handle non-finite values.
Results may differ from the reference program's by a relative error of at most 0.0049.
Values may be sent and summed in bfloat16 or wider, within the bound.
A program may use at most 64 MiB of HBM per device.

```python
import jax
import jax.numpy as jnp
from jax import lax

D = 8192
FF = 16384
BLK = 128
TOKENS = 2048
N_TOK = 16
N_HID = 32


def keep_pattern(key, tiles_r, tiles_c, split_r, split_c):
    shard_r = tiles_r // split_r
    shard_c = tiles_c // split_c
    per_shard = shard_r * shard_c
    capacity = per_shard // 2
    lowest = per_shard // 4
    shard_count = split_r * split_c
    key_count, key_pick, key_perm = jax.random.split(key, 3)
    counts = jax.random.randint(key_count, (shard_count,), lowest, capacity + 1)
    chosen = jax.random.randint(key_pick, (), 0, shard_count)
    counts = jnp.where(jnp.arange(shard_count) == chosen, capacity, counts)
    orders = jax.vmap(lambda sub_key: jax.random.permutation(sub_key, per_shard))(jax.random.split(key_perm, shard_count))
    kept = (orders < counts[:, None]).astype(jnp.int32)
    kept = kept.reshape(split_r, split_c, shard_r, shard_c).transpose(0, 2, 1, 3)
    return kept.reshape(tiles_r, tiles_c)


def draw_gate_keep(key, part):
    return keep_pattern(jax.random.fold_in(key, 11), D // BLK, FF // BLK, N_TOK, N_HID)


def draw_up_keep(key, part):
    return keep_pattern(jax.random.fold_in(key, 23), D // BLK, FF // BLK, N_TOK, N_HID)


def draw_down_keep(key, part):
    return keep_pattern(jax.random.fold_in(key, 37), FF // BLK, D // BLK, N_HID, N_TOK)


def level_of(rng, shape, cuts, low, high):
    factor_of = 1.0
    for axis_at, parts in cuts:
        heights = jax.random.uniform(jax.random.fold_in(jax.random.fold_in(rng, 6), axis_at), (parts,), jnp.float32, low / len(cuts), high / len(cuts))
        factor_of = factor_of * jnp.repeat(jnp.exp(heights), shape[axis_at] // parts).reshape((-1,) + (1,) * (len(shape) - 1 - axis_at))
    return factor_of


def scatter_about(key, extent, deviation, limit, shards=(), kind=jnp.bfloat16):
    gain = level_of(key, extent, shards, -0.22, 0.18) if shards else 1.0
    result = jax.random.normal(key, extent, jnp.float32) * deviation * gain
    return jnp.minimum(jnp.maximum(result, -limit), limit).astype(kind)


def setup_inputs(seed: int = 0) -> dict:
    keys = jax.random.split(jax.random.key(seed), 8)
    return {
        "tokens": scatter_about(keys[0], (TOKENS, D), 1.0, 6.0, ((0, 16), (1, 32))),
        "gate_weight": scatter_about(keys[1], (D, FF), (D // 2) ** -0.5, 0.09375, ((0, 16), (1, 32))),
        "up_weight": scatter_about(keys[2], (D, FF), (D // 2) ** -0.5, 0.09375, ((0, 16), (1, 32))),
        "down_weight": scatter_about(keys[3], (FF, D), (FF // 2) ** -0.5, 0.0625, ((0, 32), (1, 16))),
        "gate_keep": draw_gate_keep(jax.random.fold_in(keys[7], 71), 0),
        "up_keep": draw_up_keep(jax.random.fold_in(keys[7], 71), 0),
        "down_keep": draw_down_keep(jax.random.fold_in(keys[7], 71), 0),
    }


def prune_blocks(weight, keep_mask):
    row_count, col_count = weight.shape
    tiles = weight.reshape(row_count // BLK, BLK, col_count // BLK, BLK)
    kept = tiles * keep_mask[:, None, :, None].astype(weight.dtype)
    return kept.reshape(row_count, col_count)


def reference(tokens, gate_weight, up_weight, down_weight, gate_keep, up_keep, down_keep):
    gate_out = jnp.dot(tokens, prune_blocks(gate_weight, gate_keep), preferred_element_type=jnp.float32)
    up_out = jnp.dot(tokens, prune_blocks(up_weight, up_keep), preferred_element_type=jnp.float32)
    hidden = (jax.nn.silu(gate_out) * up_out).astype(jnp.bfloat16)
    down_pruned = prune_blocks(down_weight, down_keep)
    width_part = FF // N_HID
    hidden_parts = hidden.reshape(hidden.shape[0], N_HID, width_part).transpose(1, 0, 2)
    down_parts = down_pruned.reshape(N_HID, width_part, down_pruned.shape[1])

    def add_part(total, pieces):
        term = jnp.dot(pieces[0], pieces[1], preferred_element_type=jnp.float32)
        return total + term, None

    start = jnp.zeros((hidden.shape[0], down_pruned.shape[1]), jnp.float32)
    mixed, _ = lax.scan(add_part, start, (hidden_parts, down_parts))
    return mixed.astype(jnp.bfloat16)
```

```python
import functools

import jax
import jax.numpy as jnp
from jax import lax
from jax.experimental import pallas as pl
from jax.experimental.pallas import tpu as pltpu
from jax.sharding import PartitionSpec as P

MESH = pl.DeviceIdType.MESH
HBM = pltpu.MemorySpace.HBM
VMEM = pltpu.MemorySpace.VMEM
BF16 = jnp.bfloat16
F32 = jnp.float32

SIDE = 4
RING = 16
BLK = 128
NB = 4
CAP = 8
SHARD = NB * BLK
PACK = CAP * BLK + 16
HALF = CAP * BLK // 2


def place():
    t = lax.axis_index("tok")
    h = lax.axis_index("hid")
    return lax.rem(t, SIDE), lax.div(t, SIDE), lax.div(h, 2), lax.rem(h, 2)


def wrap(i, n):
    return lax.rem(i + n, n)


def device(x, y, z, c):
    return (y * SIDE + x, z * 2 + c)


def greet(peers):
    barrier = pltpu.get_barrier_semaphore()
    for peer in peers:
        pl.semaphore_signal(barrier, inc=1, device_id=peer, device_id_type=MESH)
    pl.semaphore_wait(barrier, len(peers))


class Gather:
    def __init__(self, buf, half, x_first, send, recv):
        x, y, z, c = place()
        self.buf, self.half, self.send, self.recv = buf, half, send, recv
        self.a, self.b = (x, y) if x_first else (y, x)
        self.slot = lambda a, b: (b * SIDE + a) if x_first else (a * SIDE + b)
        self.dev = lambda a, b: device(a, b, z, c) if x_first else device(b, a, z, c)
        self.copies = {}

    def part(self, slot, piece):
        ref = self.buf.at[slot]
        if piece is None:
            return ref
        return ref.at[self.half] if piece == 0 else ref.at[self.half2]

    def block(self, k, piece):
        a = wrap(self.a + k, SIDE)
        return a, piece

    def copy(self, key, index, slot, piece, dev):
        ref = self.part(slot, piece)
        cp = pltpu.make_async_remote_copy(
            src_ref=ref,
            dst_ref=ref,
            send_sem=self.send.at[index],
            recv_sem=self.recv.at[index],
            device_id=dev,
            device_id_type=MESH,
        )
        cp.start()
        self.copies[key] = cp

    def got(self, index, slot, piece):
        ref = self.part(slot, piece)
        x, y, z, c = place()
        pltpu.make_async_remote_copy(
            src_ref=ref,
            dst_ref=ref,
            send_sem=self.send.at[index],
            recv_sem=self.recv.at[index],
            device_id=self.dev(wrap(self.a + 1, SIDE), self.b),
            device_id_type=MESH,
        ).wait_recv()

    def first(self):
        s = self.slot(self.a, self.b)
        self.copy("r", 0, s, None, self.dev(wrap(self.a + 1, SIDE), self.b))
        self.copy("l", 1, s, None, self.dev(wrap(self.a - 1, SIDE), self.b))

    def relay(self):
        left = self.slot(wrap(self.a - 1, SIDE), self.b)
        right = self.slot(wrap(self.a + 1, SIDE), self.b)
        self.got(0, left, None)
        self.copy("fr", 2, left, 0, self.dev(wrap(self.a + 1, SIDE), self.b))
        self.got(1, right, None)
        self.copy("fl", 3, right, 1, self.dev(wrap(self.a - 1, SIDE), self.b))

    def far(self):
        opposite = self.slot(wrap(self.a + 2, SIDE), self.b)
        self.got(2, opposite, 0)
        self.got(3, opposite, 1)

    OFF = (0, -1, 1, 2)

    def second(self, i):
        a = wrap(self.a + self.OFF[i], SIDE)
        s = self.slot(a, self.b)
        self.copy(("u", i), 4 + 4 * i, s, None, self.dev(self.a, wrap(self.b + 1, SIDE)))
        self.copy(("d", i), 5 + 4 * i, s, None, self.dev(self.a, wrap(self.b - 1, SIDE)))

    def relay2(self, i):
        a = wrap(self.a + self.OFF[i], SIDE)
        below = self.slot(a, wrap(self.b - 1, SIDE))
        above = self.slot(a, wrap(self.b + 1, SIDE))
        self.got(4 + 4 * i, below, None)
        self.copy(("fu", i), 6 + 4 * i, below, 0, self.dev(self.a, wrap(self.b + 1, SIDE)))
        self.got(5 + 4 * i, above, None)
        self.copy(("fd", i), 7 + 4 * i, above, 1, self.dev(self.a, wrap(self.b - 1, SIDE)))

    def far2(self, i):
        a = wrap(self.a + self.OFF[i], SIDE)
        s = self.slot(a, wrap(self.b + 2, SIDE))
        self.got(6 + 4 * i, s, 0)
        self.got(7 + 4 * i, s, 1)

    def drain(self):
        for cp in self.copies.values():
            cp.wait_send()


def halves(gather, first, second):
    gather.half, gather.half2 = first, second
    return gather


def pack_kernel(at_ref, gk_ref, uk_ref, dk_ref, tok_ref, gw_ref, uw_ref, dw_ref, g_ref, u_ref, t_ref, d_ref):
    del at_ref
    t_ref[0] = tok_ref[...]
    lane = lax.broadcasted_iota(jnp.int32, (16, BLK), 1)
    for keep_ref, w_ref, o_ref in ((gk_ref, gw_ref, g_ref), (uk_ref, uw_ref, u_ref)):
        o_ref[...] = jnp.zeros_like(o_ref)
        rank = jnp.int32(0)
        flags = jnp.zeros((16, BLK), F32)
        for b in range(NB * NB):
            i, j = b // NB, b % NB
            keep = keep_ref[i, j]

            @pl.when(keep == 1)
            def _(i=i, j=j, rank=rank, w_ref=w_ref, o_ref=o_ref):
                row = pl.multiple_of(jnp.minimum(rank, CAP - 1) * BLK, BLK)
                o_ref[0, pl.ds(row, BLK), :] = w_ref[i * BLK : (i + 1) * BLK, j * BLK : (j + 1) * BLK]

            flags = jnp.where(lane == b, keep.astype(F32), flags)
            rank = rank + keep
        o_ref[0, CAP * BLK :, :] = flags.astype(BF16)
    for i in range(NB):
        for j in range(NB):
            r, s = slice(i * BLK, (i + 1) * BLK), slice(j * BLK, (j + 1) * BLK)
            d_ref[0, r, s] = dw_ref[r, s] * dk_ref[i, j].astype(F32).astype(BF16)


def pack(at, tokens, gw, uw, dw, gk, uk, dk):
    whole = lambda a: pl.BlockSpec(a.shape, lambda i, *_: (0,) * a.ndim)
    return pl.pallas_call(
        pack_kernel,
        grid_spec=pltpu.PrefetchScalarGridSpec(
            num_scalar_prefetch=4,
            grid=(1,),
            in_specs=[whole(a) for a in (tokens, gw, uw, dw)],
            out_specs=[
                pl.BlockSpec((1, PACK, BLK), lambda i, at, *_: (at[0], 0, 0)),
                pl.BlockSpec((1, PACK, BLK), lambda i, at, *_: (at[0], 0, 0)),
                pl.BlockSpec((1,) + tokens.shape, lambda i, at, *_: (at[1], 0, 0)),
                pl.BlockSpec((1,) + dw.shape, lambda i, at, *_: (at[2], 0, 0)),
            ],
        ),
        out_shape=[
            jax.ShapeDtypeStruct((SIDE * SIDE, PACK, BLK), BF16),
            jax.ShapeDtypeStruct((SIDE * SIDE, PACK, BLK), BF16),
            jax.ShapeDtypeStruct((2 * RING,) + tokens.shape, BF16),
            jax.ShapeDtypeStruct((2,) + dw.shape, BF16),
        ],
        name="pack",
    )(at, gk, uk, dk, tokens, gw, uw, dw)


def gather_kernel(g_in, u_in, t_in, d_in, g, u, t, d, gs, gr, us, ur, zs, zr, cs, cr, ds, dr):
    del g_in, u_in, t_in, d_in
    x, y, z, c = place()
    up, down = device(x, y, wrap(z + 1, RING), c), device(x, y, wrap(z - 1, RING), c)
    other = device(x, y, z, 1 - c)
    greet(
        (
            device(wrap(x + 1, SIDE), y, z, c),
            device(wrap(x - 1, SIDE), y, z, c),
            device(x, wrap(y + 1, SIDE), z, c),
            device(x, wrap(y - 1, SIDE), z, c),
            up,
            down,
            other,
        )
    )
    first, second = pl.ds(0, HALF), pl.ds(HALF, PACK - HALF)
    gg = halves(Gather(g, None, True, gs, gr), first, second)
    uu = halves(Gather(u, None, False, us, ur), first, second)
    sends = []

    def z_copy(block, dev, send, recv, start):
        ref = t.at[2 * block + c]
        cp = pltpu.make_async_remote_copy(
            src_ref=ref, dst_ref=ref, send_sem=send, recv_sem=recv, device_id=dev, device_id_type=MESH
        )
        if start:
            cp.start()
            sends.append(cp)
        else:
            cp.wait_recv()

    def z_step(k):
        z_copy(wrap(z - (k - 1), RING), up, zs.at[2 * k - 2], zr.at[2 * k - 2], True)
        if k < RING // 2:
            z_copy(wrap(z + (k - 1), RING), down, zs.at[2 * k - 1], zr.at[2 * k - 1], True)

    def z_wait(k):
        z_copy(wrap(z - k, RING), up, zs.at[2 * k - 2], zr.at[2 * k - 2], False)
        z_copy(wrap(z - k, RING), other, cs.at[2 * k - 1], cr.at[2 * k - 1], True)
        if k < RING // 2:
            z_copy(wrap(z + k, RING), down, zs.at[2 * k - 1], zr.at[2 * k - 1], False)
            z_copy(wrap(z + k, RING), other, cs.at[2 * k], cr.at[2 * k], True)

    def z_go(k):
        z_wait(k)
        if k < RING // 2:
            z_step(k + 1)

    z_step(1)
    gg.first()
    uu.first()
    gg.second(0)
    uu.second(0)
    z_copy(z, other, cs.at[0], cr.at[0], True)
    dref = d.at[c]
    d_copy = pltpu.make_async_remote_copy(
        src_ref=dref, dst_ref=dref, send_sem=ds.at[0], recv_sem=dr.at[0], device_id=other, device_id_type=MESH
    )
    d_copy.start()
    z_go(1)
    z_go(2)
    gg.relay()
    uu.relay()
    gg.second(1)
    uu.second(1)
    gg.second(2)
    uu.second(2)
    z_go(3)
    gg.relay2(0)
    uu.relay2(0)
    z_go(4)
    gg.far()
    uu.far()
    gg.second(3)
    uu.second(3)
    z_go(5)
    gg.relay2(1)
    uu.relay2(1)
    z_go(6)
    gg.relay2(2)
    uu.relay2(2)
    z_go(7)
    gg.far2(0)
    uu.far2(0)
    z_go(8)
    gg.relay2(3)
    uu.relay2(3)
    for i in (1, 2, 3):
        gg.far2(i)
        uu.far2(i)
    for n in range(RING):
        k = (n + 1) // 2
        block = z if n == 0 else (wrap(z - k, RING) if n % 2 else wrap(z + k, RING))
        ref = t.at[2 * block + 1 - c]
        pltpu.make_async_remote_copy(
            src_ref=ref, dst_ref=ref, send_sem=cs.at[n], recv_sem=cr.at[n], device_id=other, device_id_type=MESH
        ).wait_recv()
    oref = d.at[1 - c]
    pltpu.make_async_remote_copy(
        src_ref=oref, dst_ref=oref, send_sem=ds.at[0], recv_sem=dr.at[0], device_id=other, device_id_type=MESH
    ).wait_recv()
    d_copy.wait_send()
    gg.drain()
    uu.drain()
    for cp in sends:
        cp.wait_send()


def gather_weights(g, u, t, d):
    dma = pltpu.SemaphoreType.DMA
    arrays = (g, u, t, d)
    return pl.pallas_call(
        gather_kernel,
        out_shape=[jax.ShapeDtypeStruct(a.shape, a.dtype) for a in arrays],
        in_specs=[pl.BlockSpec(memory_space=HBM)] * 4,
        out_specs=[pl.BlockSpec(memory_space=HBM)] * 4,
        input_output_aliases={i: i for i in range(4)},
        scratch_shapes=[dma((20,))] * 4 + [dma((15,))] * 2 + [dma((16,))] * 2 + [dma((1,))] * 2,
        compiler_params=pltpu.CompilerParams(collective_id=0, has_side_effects=True),
        name="gather_weights",
    )(*arrays)


def hidden_kernel(flag_ref, at_ref, g_ref, u_ref, t_ref, own_ref, other_ref, gd, ud, ga, ua):
    s = pl.program_id(0)

    @pl.when(s == 0)
    def _():
        ga[...] = jnp.zeros_like(ga)
        ua[...] = jnp.zeros_like(ua)

    for m, (packed, dense, acc) in enumerate(((g_ref, gd, ga), (u_ref, ud, ua))):
        rank = jnp.int32(0)
        for b in range(NB * NB):
            i, j = b // NB, b % NB
            keep = flag_ref[(m * SIDE * SIDE + s) * NB * NB + b]
            row = pl.multiple_of(jnp.minimum(rank, CAP - 1) * BLK, BLK)
            tile = packed[0, pl.ds(row, BLK), :]
            dense[i * BLK : (i + 1) * BLK, j * BLK : (j + 1) * BLK] = tile * keep.astype(F32).astype(BF16)
            rank = rank + keep
        w = t_ref.shape[2]
        acc[...] += jnp.dot(t_ref[0], dense[:w], preferred_element_type=F32) + jnp.dot(
            t_ref[1], dense[w:], preferred_element_type=F32
        )

    @pl.when(s == SIDE * SIDE - 1)
    def _():
        gate = ga[...]
        hidden = (gate / (1.0 + jnp.exp(-gate)) * ua[...]).astype(BF16)
        rows = hidden.shape[0] // 2

        @pl.when(at_ref[2] == 0)
        def _():
            own_ref[0, 0] = hidden[:rows]
            other_ref[...] = hidden[rows:]

        @pl.when(at_ref[2] == 1)
        def _():
            own_ref[0, 0] = hidden[rows:]
            other_ref[...] = hidden[:rows]


def make_hidden(flags, at, g, u, t):
    rows = t.shape[1]
    return pl.pallas_call(
        hidden_kernel,
        grid_spec=pltpu.PrefetchScalarGridSpec(
            num_scalar_prefetch=2,
            grid=(SIDE * SIDE,),
            in_specs=[
                pl.BlockSpec((1, PACK, BLK), lambda s, *_: (s, 0, 0)),
                pl.BlockSpec((1, PACK, BLK), lambda s, *_: (s, 0, 0)),
                pl.BlockSpec((2,) + t.shape[1:], lambda s, *_: (s, 0, 0)),
            ],
            out_specs=[
                pl.BlockSpec((1, 1, rows // 2, SHARD), lambda s, f, at: (at[2], at[0], 0, 0)),
                pl.BlockSpec((rows // 2, SHARD), lambda s, *_: (0, 0)),
            ],
            scratch_shapes=[
                pltpu.VMEM((SHARD, SHARD), BF16),
                pltpu.VMEM((SHARD, SHARD), BF16),
                pltpu.VMEM((rows, SHARD), F32),
                pltpu.VMEM((rows, SHARD), F32),
            ],
        ),
        out_shape=[
            jax.ShapeDtypeStruct((2, SIDE * SIDE, rows // 2, SHARD), BF16),
            jax.ShapeDtypeStruct((rows // 2, SHARD), BF16),
        ],
        name="make_hidden",
    )(flags, at, g, u, t)


def spread_kernel(h_in, o_ref, h, ass, ar, bs, br, ps, pr):
    del h_in
    x, y, z, c = place()
    other = device(x, y, z, 1 - c)
    greet(
        (
            device(wrap(x + 1, SIDE), y, z, c),
            device(wrap(x - 1, SIDE), y, z, c),
            device(x, wrap(y + 1, SIDE), z, c),
            device(x, wrap(y - 1, SIDE), z, c),
            other,
        )
    )
    me = y * SIDE + x
    swap = pltpu.make_async_remote_copy(
        src_ref=o_ref,
        dst_ref=h.at[c, me],
        send_sem=ps.at[0],
        recv_sem=pr.at[0],
        device_id=other,
        device_id_type=MESH,
    )
    swap.start()
    rows = h.shape[2]
    first, second = pl.ds(0, rows // 2), pl.ds(rows // 2, rows // 2)
    aa = halves(Gather(h.at[c], None, True, ass, ar), first, second)
    bb = halves(Gather(h.at[1 - c], None, False, bs, br), first, second)
    aa.first()
    aa.second(0)
    got = h.at[1 - c, me]
    pltpu.make_async_remote_copy(
        src_ref=got, dst_ref=got, send_sem=ps.at[0], recv_sem=pr.at[0], device_id=other, device_id_type=MESH
    ).wait_recv()
    bb.first()
    bb.second(0)
    aa.relay()
    aa.second(1)
    aa.second(2)
    bb.relay()
    bb.second(1)
    bb.second(2)
    aa.relay2(0)
    bb.relay2(0)
    aa.far()
    aa.second(3)
    bb.far()
    bb.second(3)
    for i in (1, 2, 3):
        aa.relay2(i)
        bb.relay2(i)
    for i in range(4):
        aa.far2(i)
        bb.far2(i)
    swap.wait_send()
    aa.drain()
    bb.drain()


def spread_hidden(h, other):
    dma = pltpu.SemaphoreType.DMA
    return pl.pallas_call(
        spread_kernel,
        out_shape=jax.ShapeDtypeStruct(h.shape, h.dtype),
        in_specs=[pl.BlockSpec(memory_space=HBM)] * 2,
        out_specs=pl.BlockSpec(memory_space=HBM),
        input_output_aliases={0: 0},
        scratch_shapes=[dma((20,))] * 4 + [dma((1,))] * 2,
        compiler_params=pltpu.CompilerParams(collective_id=1, has_side_effects=True),
        name="spread_hidden",
    )(h, other)


PARTS = 2


def reduce_kernel(h_ref, d_ref, o_ref, p, up_buf, down_buf, us, ur, ds, dr):
    x, y, z, c = place()
    up, down = device(x, y, wrap(z + 1, RING), c), device(x, y, wrap(z - 1, RING), c)
    greet((up, down))
    blocks, rows = h_ref.shape[1], h_ref.shape[2]
    group = 4

    @pl.loop(0, blocks // group)
    def _(i):
        at = pl.ds(i * group, group)
        width = h_ref.shape[3]
        own = h_ref[0, at].reshape(group * rows, width)
        far = h_ref[1, at].reshape(group * rows, width)
        sums = jnp.dot(own, d_ref[0], preferred_element_type=F32) + jnp.dot(
            far, d_ref[1], preferred_element_type=F32
        )
        p[at] = sums.reshape(group, rows, d_ref.shape[2])

    far_up, far_down = RING // 2, RING // 2 - 1
    piece = rows // PARTS

    def send(buf, step, q, dev, ss, rs, src):
        cp = pltpu.make_async_remote_copy(
            src_ref=src,
            dst_ref=buf.at[step, q],
            send_sem=ss.at[step * PARTS + q],
            recv_sem=rs.at[step * PARTS + q],
            device_id=dev,
            device_id_type=MESH,
        )
        return cp

    sends = []
    for q in range(PARTS):
        r = pl.ds(q * piece, piece)
        a = send(up_buf, 0, q, up, us, ur, p.at[wrap(z + far_up, RING), r])
        a.start()
        b = send(down_buf, 0, q, down, ds, dr, p.at[wrap(z - far_down, RING), r])
        b.start()
        sends += [a, b]
    for step in range(1, far_up + 1):
        for q in range(PARTS):
            r = pl.ds(q * piece, piece)
            send(up_buf, step - 1, q, up, us, ur, up_buf.at[step - 1, q]).wait_recv()
            if step < far_up:
                up_buf[step - 1, q] += p[wrap(z + far_up - step, RING), r]
                a = send(up_buf, step, q, up, us, ur, up_buf.at[step - 1, q])
                a.start()
                sends.append(a)
            if step <= far_down:
                send(down_buf, step - 1, q, down, ds, dr, down_buf.at[step - 1, q]).wait_recv()
                if step < far_down:
                    down_buf[step - 1, q] += p[wrap(z - far_down + step, RING), r]
                    b = send(down_buf, step, q, down, ds, dr, down_buf.at[step - 1, q])
                    b.start()
                    sends.append(b)
            if step == far_up:
                total = p[z, r] + up_buf[far_up - 1, q] + down_buf[far_down - 1, q]
                o_ref[r, :] = total.astype(BF16)
    for cp in sends:
        cp.wait_send()


def reduce_sums(h, d):
    dma = pltpu.SemaphoreType.DMA
    _, blocks, rows, _ = h.shape
    cols = d.shape[2]
    n_up, n_down = RING // 2, RING // 2 - 1
    return pl.pallas_call(
        reduce_kernel,
        out_shape=jax.ShapeDtypeStruct((rows, cols), BF16),
        in_specs=[pl.BlockSpec(memory_space=VMEM)] * 2,
        out_specs=pl.BlockSpec(memory_space=VMEM),
        scratch_shapes=[
            pltpu.VMEM((blocks, rows, cols), F32),
            pltpu.VMEM((n_up, PARTS, rows // PARTS, cols), F32),
            pltpu.VMEM((n_down, PARTS, rows // PARTS, cols), F32),
            dma((n_up * PARTS,)),
            dma((n_up * PARTS,)),
            dma((n_down * PARTS,)),
            dma((n_down * PARTS,)),
        ],
        compiler_params=pltpu.CompilerParams(collective_id=2, has_side_effects=True, vmem_limit_bytes=32 << 20),
        name="reduce_sums",
    )(h, d)


def local(tokens, gate_weight, up_weight, down_weight, gate_keep, up_keep, down_keep):
    t = lax.axis_index("tok")
    h = lax.axis_index("hid")
    at = jnp.stack([t, h, lax.rem(h, 2)]).astype(jnp.int32)
    g, u, x, d = pack(at, tokens, gate_weight, up_weight, down_weight, gate_keep, up_keep, down_keep)
    g, u, x, d = gather_weights(g, u, x, d)
    flags = jnp.stack([g[:, CAP * BLK, : NB * NB], u[:, CAP * BLK, : NB * NB]])
    flags = flags.astype(F32).astype(jnp.int32).reshape(-1)
    own, other = make_hidden(flags, at, g, u, x)
    hidden = spread_hidden(own, other)
    return reduce_sums(hidden, d)


def solution(mesh):
    return jax.shard_map(
        local,
        mesh=mesh,
        in_specs=(
            P("tok", "hid"),
            P("tok", "hid"),
            P("tok", "hid"),
            P("hid", "tok"),
            P("tok", "hid"),
            P("tok", "hid"),
            P("hid", "tok"),
        ),
        out_specs=P("hid", "tok"),
        check_vma=False,
    )
```

```python
import functools

import jax
import jax.numpy as jnp
from jax import lax
from jax.experimental import pallas as pl
from jax.experimental.pallas import tpu as pltpu
from jax.sharding import PartitionSpec as P

MESH = pl.DeviceIdType.MESH
HBM = pltpu.MemorySpace.HBM
VMEM = pltpu.MemorySpace.VMEM
BF16 = jnp.bfloat16
F32 = jnp.float32

SIDE = 4
RING = 16
BLK = 128
NB = 4
CAP = 8
SHARD = NB * BLK
PACK = CAP * BLK


def place():
    t = lax.axis_index("tok")
    h = lax.axis_index("hid")
    return lax.rem(t, SIDE), lax.div(t, SIDE), lax.div(h, 2), lax.rem(h, 2)


def wrap(i, n):
    return lax.rem(i + n, n)


def device(x, y, z, c):
    return (y * SIDE + x, z * 2 + c)


def greet(peers):
    barrier = pltpu.get_barrier_semaphore()
    for peer in peers:
        pl.semaphore_signal(barrier, inc=1, device_id=peer, device_id_type=MESH)
    pl.semaphore_wait(barrier, len(peers))


class Gather:
    def __init__(self, buf, rows, x_first, send, recv):
        x, y, z, c = place()
        self.buf, self.send, self.recv = buf, send, recv
        self.split = rows > 1
        self.pieces = (pl.ds(0, rows // 2), pl.ds(rows // 2, rows // 2))
        self.a, self.b = (x, y) if x_first else (y, x)
        self.slot = lambda a, b: (b * SIDE + a) if x_first else (a * SIDE + b)
        self.dev = lambda a, b: device(a, b, z, c) if x_first else device(b, a, z, c)
        self.copies = {}

    def part(self, slot, piece):
        ref = self.buf.at[slot]
        if piece is None:
            return ref
        return ref.at[self.pieces[piece]]

    def copy(self, key, index, slot, piece, dev):
        ref = self.part(slot, piece)
        cp = pltpu.make_async_remote_copy(
            src_ref=ref,
            dst_ref=ref,
            send_sem=self.send.at[index],
            recv_sem=self.recv.at[index],
            device_id=dev,
            device_id_type=MESH,
        )
        cp.start()
        self.copies[key] = cp

    def got(self, index, slot, piece):
        ref = self.part(slot, piece)
        x, y, z, c = place()
        pltpu.make_async_remote_copy(
            src_ref=ref,
            dst_ref=ref,
            send_sem=self.send.at[index],
            recv_sem=self.recv.at[index],
            device_id=self.dev(wrap(self.a + 1, SIDE), self.b),
            device_id_type=MESH,
        ).wait_recv()

    def first(self):
        s = self.slot(self.a, self.b)
        self.copy("r", 0, s, None, self.dev(wrap(self.a + 1, SIDE), self.b))
        self.copy("l", 1, s, None, self.dev(wrap(self.a - 1, SIDE), self.b))

    def relay(self):
        left = self.slot(wrap(self.a - 1, SIDE), self.b)
        right = self.slot(wrap(self.a + 1, SIDE), self.b)
        self.got(0, left, None)
        self.copy("fr", 2, left, 0 if self.split else None, self.dev(wrap(self.a + 1, SIDE), self.b))
        self.got(1, right, None)
        if self.split:
            self.copy("fl", 3, right, 1, self.dev(wrap(self.a - 1, SIDE), self.b))

    def far(self):
        opposite = self.slot(wrap(self.a + 2, SIDE), self.b)
        self.got(2, opposite, 0 if self.split else None)
        if self.split:
            self.got(3, opposite, 1)

    OFF = (0, -1, 1, 2)

    def second(self, i):
        a = wrap(self.a + self.OFF[i], SIDE)
        s = self.slot(a, self.b)
        self.copy(("u", i), 4 + 4 * i, s, None, self.dev(self.a, wrap(self.b + 1, SIDE)))
        self.copy(("d", i), 5 + 4 * i, s, None, self.dev(self.a, wrap(self.b - 1, SIDE)))

    def relay2(self, i):
        a = wrap(self.a + self.OFF[i], SIDE)
        below = self.slot(a, wrap(self.b - 1, SIDE))
        above = self.slot(a, wrap(self.b + 1, SIDE))
        self.got(4 + 4 * i, below, None)
        self.copy(("fu", i), 6 + 4 * i, below, 0 if self.split else None, self.dev(self.a, wrap(self.b + 1, SIDE)))
        self.got(5 + 4 * i, above, None)
        if self.split:
            self.copy(("fd", i), 7 + 4 * i, above, 1, self.dev(self.a, wrap(self.b - 1, SIDE)))

    def far2(self, i):
        a = wrap(self.a + self.OFF[i], SIDE)
        s = self.slot(a, wrap(self.b + 2, SIDE))
        self.got(6 + 4 * i, s, 0 if self.split else None)
        if self.split:
            self.got(7 + 4 * i, s, 1)

    def drain(self):
        for cp in self.copies.values():
            cp.wait_send()


def pack_kernel(gk_ref, uk_ref, dk_ref, gw_ref, uw_ref, dw_ref, m_ref, g_ref, u_ref, d_ref):
    lane = lax.broadcasted_iota(jnp.int32, m_ref.shape, 1)
    flags = jnp.zeros(m_ref.shape, jnp.int32)
    for m, (keep_ref, w_ref, o_ref) in enumerate(((gk_ref, gw_ref, g_ref), (uk_ref, uw_ref, u_ref))):
        o_ref[...] = jnp.zeros_like(o_ref)
        rank = jnp.int32(0)
        for b in range(NB * NB):
            i, j = b // NB, b % NB
            keep = keep_ref[i, j]

            @pl.when(keep == 1)
            def _(i=i, j=j, rank=rank, w_ref=w_ref, o_ref=o_ref):
                row = pl.multiple_of(jnp.minimum(rank, CAP - 1) * BLK, BLK)
                o_ref[pl.ds(row, BLK), :] = w_ref[i * BLK : (i + 1) * BLK, j * BLK : (j + 1) * BLK]

            flags = jnp.where(lane == m * NB * NB + b, keep, flags)
            rank = rank + keep
    m_ref[...] = flags
    for i in range(NB):
        for j in range(NB):
            r, s = slice(i * BLK, (i + 1) * BLK), slice(j * BLK, (j + 1) * BLK)
            d_ref[r, s] = dw_ref[r, s] * dk_ref[i, j].astype(F32).astype(BF16)


def pack(gw, uw, dw, gk, uk, dk):
    return pl.pallas_call(
        pack_kernel,
        in_specs=[pl.BlockSpec(memory_space=pltpu.MemorySpace.SMEM)] * 3 + [pl.BlockSpec(memory_space=VMEM)] * 3,
        out_specs=[pl.BlockSpec(memory_space=VMEM)] * 4,
        out_shape=[
            jax.ShapeDtypeStruct((1, BLK), jnp.int32),
            jax.ShapeDtypeStruct((PACK, BLK), BF16),
            jax.ShapeDtypeStruct((PACK, BLK), BF16),
            jax.ShapeDtypeStruct(dw.shape, BF16),
        ],
        name="pack",
    )(gk, uk, dk, gw, uw, dw)


def remote(src, dst, send, recv, dev):
    return pltpu.make_async_remote_copy(
        src_ref=src, dst_ref=dst, send_sem=send, recv_sem=recv, device_id=dev, device_id_type=MESH
    )


def hidden_kernel(
    m_in, g_in, u_in, t_in, d_in, hid, far_d, m, g, u, t, gp, up_, gd, ud, ga, ua, flags,
    gs, gr, us, ur, ms, mr, zs, zr, cs, cr, ds, dr, ls,
):
    x, y, z, c = place()
    me, h = y * SIDE + x, z * 2 + c
    up, down = device(x, y, wrap(z + 1, RING), c), device(x, y, wrap(z - 1, RING), c)
    other = device(x, y, z, 1 - c)
    own = [
        pltpu.make_async_copy(src, dst, ls.at[i])
        for i, (src, dst) in enumerate(((t_in, t.at[h]), (g_in, g.at[me]), (u_in, u.at[me]), (m_in, m.at[me])))
    ]
    for cp in own:
        cp.start()
    greet(
        (
            device(wrap(x + 1, SIDE), y, z, c),
            device(wrap(x - 1, SIDE), y, z, c),
            device(x, wrap(y + 1, SIDE), z, c),
            device(x, wrap(y - 1, SIDE), z, c),
            up,
            down,
            other,
        )
    )
    for cp in own:
        cp.wait()
    gg = Gather(g, PACK, True, gs, gr)
    uu = Gather(u, PACK, False, us, ur)
    mm = Gather(m, 1, True, ms, mr)
    sends = []

    def z_copy(block, dev, send, recv, start):
        ref = t.at[2 * block + c]
        cp = remote(ref, ref, send, recv, dev)
        if start:
            cp.start()
            sends.append(cp)
        else:
            cp.wait_recv()

    def z_step(k):
        z_copy(wrap(z - (k - 1), RING), up, zs.at[2 * k - 2], zr.at[2 * k - 2], True)
        if k < RING // 2:
            z_copy(wrap(z + (k - 1), RING), down, zs.at[2 * k - 1], zr.at[2 * k - 1], True)

    def z_wait(k):
        z_copy(wrap(z - k, RING), up, zs.at[2 * k - 2], zr.at[2 * k - 2], False)
        if k < RING // 2:
            z_copy(wrap(z + k, RING), down, zs.at[2 * k - 1], zr.at[2 * k - 1], False)

    def z_share(k):
        z_copy(wrap(z - k, RING), other, cs.at[2 * k - 1], cr.at[2 * k - 1], True)
        if k < RING // 2:
            z_copy(wrap(z + k, RING), other, cs.at[2 * k], cr.at[2 * k], True)

    def z_go(k):
        z_wait(k)
        if k < RING // 2:
            z_step(k + 1)
        z_share(k)

    z_step(1)
    mm.first()
    mm.second(0)
    gg.first()
    uu.first()
    gg.second(0)
    uu.second(0)
    z_copy(z, other, cs.at[0], cr.at[0], True)
    d_copy = remote(d_in, far_d, ds.at[0], dr.at[0], other)
    d_copy.start()
    mm.relay()
    mm.second(1)
    mm.second(2)
    z_go(1)
    mm.relay2(0)
    mm.far()
    mm.second(3)
    z_go(2)
    gg.relay()
    uu.relay()
    gg.second(1)
    uu.second(1)
    gg.second(2)
    uu.second(2)
    for i in (1, 2, 3):
        mm.relay2(i)
    z_go(3)
    gg.relay2(0)
    uu.relay2(0)
    z_go(4)
    gg.far()
    uu.far()
    gg.second(3)
    uu.second(3)
    for i in range(4):
        mm.far2(i)
    z_go(5)
    gg.relay2(1)
    uu.relay2(1)
    z_go(6)
    gg.relay2(2)
    uu.relay2(2)
    flag_copy = pltpu.make_async_copy(m, flags, ls.at[4])
    flag_copy.start()
    ga[...] = jnp.zeros_like(ga)
    ua[...] = jnp.zeros_like(ua)
    z_go(7)
    z_go(8)
    for n in range(RING):
        k = (n + 1) // 2
        block = z if n == 0 else (wrap(z - k, RING) if n % 2 else wrap(z + k, RING))
        ref = t.at[2 * block + 1 - c]
        remote(ref, ref, cs.at[n], cr.at[n], other).wait_recv()
    flag_copy.wait()

    def shard(dx, dy):
        s = wrap(y + dy, SIDE) * SIDE + wrap(x + dx, SIDE)
        w = t.shape[2]
        for k, (buf, stage, dense, acc) in enumerate(((g, gp, gd, ga), (u, up_, ud, ua))):
            stage[...] = buf[s].reshape(stage.shape)
            rank = jnp.int32(0)
            for b in range(NB * NB):
                i, j = b // NB, b % NB
                keep = flags[s, 0, k * NB * NB + b]
                tile = stage[jnp.minimum(rank, CAP - 1)]
                dense[i * BLK : (i + 1) * BLK, j * BLK : (j + 1) * BLK] = tile * keep.astype(F32).astype(BF16)
                rank = rank + keep
            acc[...] += jnp.dot(t[2 * s], dense[:w], preferred_element_type=F32) + jnp.dot(
                t[2 * s + 1], dense[w:], preferred_element_type=F32
            )

    @pl.loop(0, 5)
    def _(n):
        sign = (1 - 2 * lax.rem(n + 1, 2)) * lax.div(n + 3, 4)
        on_x = 1 - lax.div(n, 3)
        shard(sign * on_x, sign * (1 - on_x))

    gg.relay2(3)
    uu.relay2(3)

    @pl.loop(0, 4)
    def _(n):
        shard(1 - 2 * lax.rem(n, 2), 1 - 2 * lax.div(n, 2))

    gg.far2(0)
    uu.far2(0)

    @pl.loop(0, 2)
    def _(n):
        shard(2 * n, 2 * (1 - n))

    for i in (1, 2):
        gg.far2(i)
        uu.far2(i)

    @pl.loop(0, 4)
    def _(n):
        sign = 1 - 2 * lax.rem(n, 2)
        on_x = lax.div(n, 2)
        shard(2 * on_x + sign * (1 - on_x), sign * on_x + 2 * (1 - on_x))

    gg.far2(3)
    uu.far2(3)
    shard(2, 2)
    gate = ga[...]
    hidden = (gate / (1.0 + jnp.exp(-gate)) * ua[...]).astype(BF16)
    hid[...] = hidden.reshape(hid.shape)
    remote(d_in, far_d, ds.at[0], dr.at[0], other).wait_recv()
    d_copy.wait_send()
    mm.drain()
    gg.drain()
    uu.drain()
    for cp in sends:
        cp.wait_send()


def make_hidden(m, g, u, t, d):
    dma = pltpu.SemaphoreType.DMA
    rows, width = t.shape
    chips = SIDE * SIDE
    hid, far_d, _ = pl.pallas_call(
        hidden_kernel,
        out_shape=[
            jax.ShapeDtypeStruct((2, rows // 2, SHARD), BF16),
            jax.ShapeDtypeStruct(d.shape, BF16),
            jax.ShapeDtypeStruct((chips,) + m.shape, m.dtype),
        ],
        in_specs=[pl.BlockSpec(memory_space=HBM)] * 5,
        out_specs=[
            pl.BlockSpec(memory_space=VMEM),
            pl.BlockSpec(memory_space=HBM),
            pl.BlockSpec(memory_space=HBM),
        ],
        scratch_shapes=[
            pltpu.VMEM((chips, PACK, BLK), BF16),
            pltpu.VMEM((chips, PACK, BLK), BF16),
            pltpu.VMEM((2 * RING, rows, width), BF16),
            pltpu.VMEM((CAP, BLK, BLK), BF16),
            pltpu.VMEM((CAP, BLK, BLK), BF16),
            pltpu.VMEM((SHARD, SHARD), BF16),
            pltpu.VMEM((SHARD, SHARD), BF16),
            pltpu.VMEM((rows, SHARD), F32),
            pltpu.VMEM((rows, SHARD), F32),
            pltpu.SMEM((chips,) + m.shape, jnp.int32),
        ]
        + [dma((20,))] * 6
        + [dma((15,))] * 2
        + [dma((16,))] * 2
        + [dma((1,))] * 2
        + [dma((5,))],
        compiler_params=pltpu.CompilerParams(collective_id=0, has_side_effects=True, vmem_limit_bytes=48 << 20),
        name="make_hidden",
    )(m, g, u, t, d)
    return hid, far_d


PARTS = 2


def tail_kernel(
    hid, d_own, d_far, o_ref, ha, hb, p, up_buf, down_buf,
    as0, ar0, as1, ar1, bs0, br0, bs1, br1, ps, pr, us, ur, ds, dr, ls,
):
    x, y, z, c = place()
    up, down = device(x, y, wrap(z + 1, RING), c), device(x, y, wrap(z - 1, RING), c)
    other = device(x, y, z, 1 - c)
    me = y * SIDE + x
    piece = ha.shape[2]
    own = [
        pltpu.make_async_copy(hid.at[c, pl.ds(q * piece, piece)], ha.at[q, me], ls.at[q]) for q in range(PARTS)
    ]
    for cp in own:
        cp.start()
    greet(
        (
            device(wrap(x + 1, SIDE), y, z, c),
            device(wrap(x - 1, SIDE), y, z, c),
            device(x, wrap(y + 1, SIDE), z, c),
            device(x, wrap(y - 1, SIDE), z, c),
            up,
            down,
            other,
        )
    )
    swaps = [
        remote(hid.at[1 - c, pl.ds(q * piece, piece)], hb.at[q, me], ps.at[q], pr.at[q], other) for q in range(PARTS)
    ]
    for cp in swaps:
        cp.start()
    for cp in own:
        cp.wait()
    a = [Gather(ha.at[q], piece, True, s, r) for q, (s, r) in enumerate(((as0, ar0), (as1, ar1)))]
    b = [Gather(hb.at[q], piece, False, s, r) for q, (s, r) in enumerate(((bs0, br0), (bs1, br1)))]
    sends = []
    far_up, far_down = RING // 2, RING // 2 - 1

    def begin(q):
        a[q].first()
        a[q].second(0)
        swaps[q].wait_recv()
        b[q].first()
        b[q].second(0)

    def near(q):
        for s in (a[q], b[q]):
            s.relay()
            s.second(1)
            s.second(2)

    def middle(q):
        for s in (a[q], b[q]):
            s.relay2(0)
        for s in (a[q], b[q]):
            s.far()
            s.second(3)

    def late(q):
        for i in (1, 2, 3):
            for s in (a[q], b[q]):
                s.relay2(i)

    def end(q):
        for i in range(4):
            for s in (a[q], b[q]):
                s.far2(i)

    def multiply(q):
        blocks, _, width = ha.shape[1:]
        left = ha[q].reshape(blocks * piece, width)
        right = hb[q].reshape(blocks * piece, width)
        sums = jnp.dot(left, d_own[...], preferred_element_type=F32) + jnp.dot(
            right, d_far[...], preferred_element_type=F32
        )
        p[q] = sums.reshape(p.shape[1:])

    def ring(buf, step, q, dev, ss, rs, src):
        n = step * PARTS + q
        return remote(src, buf.at[step, q], ss.at[n], rs.at[n], dev)

    def push(q):
        for buf, dev, ss, rs, block in (
            (up_buf, up, us, ur, wrap(z + far_up, RING)),
            (down_buf, down, ds, dr, wrap(z - far_down, RING)),
        ):
            cp = ring(buf, 0, q, dev, ss, rs, p.at[q, block])
            cp.start()
            sends.append(cp)

    def step(k, q):
        for buf, dev, ss, rs, far, block in (
            (up_buf, up, us, ur, far_up, wrap(z + far_up - k, RING)),
            (down_buf, down, ds, dr, far_down, wrap(z - far_down + k, RING)),
        ):
            if k > far:
                continue
            here = buf.at[k - 1, q]
            ring(buf, k - 1, q, dev, ss, rs, here).wait_recv()
            if k < far:
                buf[k - 1, q] += p[q, block]
                cp = ring(buf, k, q, dev, ss, rs, here)
                cp.start()
                sends.append(cp)
        if k == far_up:
            total = p[q, z] + up_buf[far_up - 1, q] + down_buf[far_down - 1, q]
            o_ref[q * piece : (q + 1) * piece, :] = total.astype(BF16)

    begin(0)
    near(0)
    begin(1)
    middle(0)
    near(1)
    late(0)
    middle(1)
    end(0)
    multiply(0)
    push(0)
    late(1)
    step(1, 0)
    end(1)
    multiply(1)
    push(1)
    for k in range(2, far_up + 1):
        step(k, 0)
        step(k - 1, 1)
    step(far_up, 1)
    for cp in swaps:
        cp.wait_send()
    for s in a + b:
        s.drain()
    for cp in sends:
        cp.wait_send()


def tail(hid, d_own, d_far):
    dma = pltpu.SemaphoreType.DMA
    _, rows, width = hid.shape
    cols = d_own.shape[1]
    chips = SIDE * SIDE
    n_up, n_down = RING // 2, RING // 2 - 1
    piece = rows // PARTS
    return pl.pallas_call(
        tail_kernel,
        out_shape=jax.ShapeDtypeStruct((rows, cols), BF16),
        in_specs=[pl.BlockSpec(memory_space=HBM)] + [pl.BlockSpec(memory_space=VMEM)] * 2,
        out_specs=pl.BlockSpec(memory_space=VMEM),
        scratch_shapes=[
            pltpu.VMEM((PARTS, chips, piece, width), BF16),
            pltpu.VMEM((PARTS, chips, piece, width), BF16),
            pltpu.VMEM((PARTS, chips, piece, cols), F32),
            pltpu.VMEM((n_up, PARTS, piece, cols), F32),
            pltpu.VMEM((n_down, PARTS, piece, cols), F32),
        ]
        + [dma((20,))] * 8
        + [dma((PARTS,))] * 2
        + [dma((n_up * PARTS,))] * 2
        + [dma((n_down * PARTS,))] * 2
        + [dma((PARTS,))],
        compiler_params=pltpu.CompilerParams(collective_id=1, has_side_effects=True, vmem_limit_bytes=48 << 20),
        name="tail",
    )(hid, d_own, d_far)


def local(tokens, gate_weight, up_weight, down_weight, gate_keep, up_keep, down_keep):
    m, g, u, d = pack(gate_weight, up_weight, down_weight, gate_keep, up_keep, down_keep)
    hid, far_d = make_hidden(m, g, u, tokens, d)
    return tail(hid, d, far_d)


def solution(mesh):
    return jax.shard_map(
        local,
        mesh=mesh,
        in_specs=(
            P("tok", "hid"),
            P("tok", "hid"),
            P("tok", "hid"),
            P("hid", "tok"),
            P("tok", "hid"),
            P("tok", "hid"),
            P("hid", "tok"),
        ),
        out_specs=P("hid", "tok"),
        check_vma=False,
    )
```

```python
import functools

import jax
import jax.numpy as jnp
from jax import lax
from jax.experimental import pallas as pl
from jax.experimental.pallas import tpu as pltpu
from jax.sharding import PartitionSpec as P

MESH = pl.DeviceIdType.MESH
HBM = pltpu.MemorySpace.HBM
VMEM = pltpu.MemorySpace.VMEM
BF16 = jnp.bfloat16
F32 = jnp.float32

SIDE = 4
RING = 16
BLK = 128
NB = 4
CAP = 8
SHARD = NB * BLK
PACK = CAP * BLK


def place():
    t = lax.axis_index("tok")
    h = lax.axis_index("hid")
    return lax.rem(t, SIDE), lax.div(t, SIDE), lax.div(h, 2), lax.rem(h, 2)


def wrap(i, n):
    return lax.rem(i + n, n)


def device(x, y, z, c):
    return (y * SIDE + x, z * 2 + c)


def greet(peers):
    barrier = pltpu.get_barrier_semaphore()
    for peer in peers:
        pl.semaphore_signal(barrier, inc=1, device_id=peer, device_id_type=MESH)
    pl.semaphore_wait(barrier, len(peers))


class Gather:
    def __init__(self, buf, rows, x_first, send, recv):
        x, y, z, c = place()
        self.buf, self.send, self.recv = buf, send, recv
        self.split = rows > 1
        self.pieces = (pl.ds(0, rows // 2), pl.ds(rows // 2, rows // 2))
        self.a, self.b = (x, y) if x_first else (y, x)
        self.slot = lambda a, b: (b * SIDE + a) if x_first else (a * SIDE + b)
        self.dev = lambda a, b: device(a, b, z, c) if x_first else device(b, a, z, c)
        self.copies = {}

    def part(self, slot, piece):
        ref = self.buf.at[slot]
        if piece is None:
            return ref
        return ref.at[self.pieces[piece]]

    def copy(self, key, index, slot, piece, dev):
        ref = self.part(slot, piece)
        cp = pltpu.make_async_remote_copy(
            src_ref=ref,
            dst_ref=ref,
            send_sem=self.send.at[index],
            recv_sem=self.recv.at[index],
            device_id=dev,
            device_id_type=MESH,
        )
        cp.start()
        self.copies[key] = cp

    def got(self, index, slot, piece):
        ref = self.part(slot, piece)
        x, y, z, c = place()
        pltpu.make_async_remote_copy(
            src_ref=ref,
            dst_ref=ref,
            send_sem=self.send.at[index],
            recv_sem=self.recv.at[index],
            device_id=self.dev(wrap(self.a + 1, SIDE), self.b),
            device_id_type=MESH,
        ).wait_recv()

    def first(self):
        s = self.slot(self.a, self.b)
        self.copy("r", 0, s, None, self.dev(wrap(self.a + 1, SIDE), self.b))
        self.copy("l", 1, s, None, self.dev(wrap(self.a - 1, SIDE), self.b))

    def relay(self):
        left = self.slot(wrap(self.a - 1, SIDE), self.b)
        right = self.slot(wrap(self.a + 1, SIDE), self.b)
        self.got(0, left, None)
        self.copy("fr", 2, left, 0 if self.split else None, self.dev(wrap(self.a + 1, SIDE), self.b))
        self.got(1, right, None)
        if self.split:
            self.copy("fl", 3, right, 1, self.dev(wrap(self.a - 1, SIDE), self.b))

    def far(self):
        opposite = self.slot(wrap(self.a + 2, SIDE), self.b)
        self.got(2, opposite, 0 if self.split else None)
        if self.split:
            self.got(3, opposite, 1)

    OFF = (0, -1, 1, 2)

    def second(self, i):
        a = wrap(self.a + self.OFF[i], SIDE)
        s = self.slot(a, self.b)
        self.copy(("u", i), 4 + 4 * i, s, None, self.dev(self.a, wrap(self.b + 1, SIDE)))
        self.copy(("d", i), 5 + 4 * i, s, None, self.dev(self.a, wrap(self.b - 1, SIDE)))

    def relay2(self, i):
        a = wrap(self.a + self.OFF[i], SIDE)
        below = self.slot(a, wrap(self.b - 1, SIDE))
        above = self.slot(a, wrap(self.b + 1, SIDE))
        self.got(4 + 4 * i, below, None)
        self.copy(("fu", i), 6 + 4 * i, below, 0 if self.split else None, self.dev(self.a, wrap(self.b + 1, SIDE)))
        self.got(5 + 4 * i, above, None)
        if self.split:
            self.copy(("fd", i), 7 + 4 * i, above, 1, self.dev(self.a, wrap(self.b - 1, SIDE)))

    def far2(self, i):
        a = wrap(self.a + self.OFF[i], SIDE)
        s = self.slot(a, wrap(self.b + 2, SIDE))
        self.got(6 + 4 * i, s, 0 if self.split else None)
        if self.split:
            self.got(7 + 4 * i, s, 1)

    def drain(self):
        for cp in self.copies.values():
            cp.wait_send()


def pack_kernel(gk_ref, uk_ref, dk_ref, gw_ref, uw_ref, dw_ref, m_ref, g_ref, u_ref, d_ref):
    lane = lax.broadcasted_iota(jnp.int32, m_ref.shape, 1)
    flags = jnp.zeros(m_ref.shape, jnp.int32)
    for m, (keep_ref, w_ref, o_ref) in enumerate(((gk_ref, gw_ref, g_ref), (uk_ref, uw_ref, u_ref))):
        o_ref[...] = jnp.zeros_like(o_ref)
        rank = jnp.int32(0)
        for b in range(NB * NB):
            i, j = b // NB, b % NB
            keep = keep_ref[i, j]

            @pl.when(keep == 1)
            def _(i=i, j=j, rank=rank, w_ref=w_ref, o_ref=o_ref):
                row = pl.multiple_of(jnp.minimum(rank, CAP - 1) * BLK, BLK)
                o_ref[pl.ds(row, BLK), :] = w_ref[i * BLK : (i + 1) * BLK, j * BLK : (j + 1) * BLK]

            flags = jnp.where(lane == m * NB * NB + b, keep, flags)
            rank = rank + keep
    m_ref[...] = flags
    for i in range(NB):
        for j in range(NB):
            r, s = slice(i * BLK, (i + 1) * BLK), slice(j * BLK, (j + 1) * BLK)
            d_ref[r, s] = dw_ref[r, s] * dk_ref[i, j].astype(F32).astype(BF16)


def pack(gw, uw, dw, gk, uk, dk):
    return pl.pallas_call(
        pack_kernel,
        in_specs=[pl.BlockSpec(memory_space=pltpu.MemorySpace.SMEM)] * 3 + [pl.BlockSpec(memory_space=VMEM)] * 3,
        out_specs=[pl.BlockSpec(memory_space=VMEM)] * 4,
        out_shape=[
            jax.ShapeDtypeStruct((1, BLK), jnp.int32),
            jax.ShapeDtypeStruct((PACK, BLK), BF16),
            jax.ShapeDtypeStruct((PACK, BLK), BF16),
            jax.ShapeDtypeStruct(dw.shape, BF16),
        ],
        name="pack",
    )(gk, uk, dk, gw, uw, dw)


def remote(src, dst, send, recv, dev):
    return pltpu.make_async_remote_copy(
        src_ref=src, dst_ref=dst, send_sem=send, recv_sem=recv, device_id=dev, device_id_type=MESH
    )


class Line(Gather):
    def __init__(self, buf, rows, along_x, send, recv):
        super().__init__(buf, rows, along_x, send, recv)
        self.slot = lambda a, b: a


class Product:
    def __init__(self, split_x, refs):
        x, y, z, c = place()
        self.a, self.b = (x, y) if split_x else (y, x)
        self.dev = lambda a: device(a, y, z, c) if split_x else device(x, a, z, c)
        self.part = (lambda s: (lax.rem(s, SIDE), lax.div(s, SIDE))) if split_x else (
            lambda s: (lax.div(s, SIDE), lax.rem(s, SIDE))
        )
        (self.w, self.m, self.t, self.acc, self.far_in, self.near_in, self.flags) = refs[:7]
        ws, wr, ms, mr, self.ts, self.tr, self.tl, self.hs, self.hr, self.rs, self.rr = refs[7:]
        self.lane = 0 if split_x else NB * NB
        self.weights = Line(self.w, PACK, not split_x, ws, wr)
        self.masks = Line(self.m, 1, not split_x, ms, mr)

    def block(self, j):
        return self.t.at[j, place()[3], self.a]

    def dispatch(self, src, s):
        to, j = self.part(s)
        off = wrap(to - self.a, SIDE)

        @pl.when(off == 0)
        def _():
            pltpu.make_async_copy(src, self.block(j), self.tl.at[j]).start()

        @pl.when(off != 0)
        def _():
            remote(src, self.block(j), self.ts.at[j, off], self.tr.at[j, off], self.dev(to)).start()

    def collect(self, s, other):
        to, j = self.part(s)

        @pl.when(to == self.a)
        def _():
            ref = self.block(j)
            pltpu.make_async_copy(ref, ref, self.tl.at[j]).wait()
            for off in range(1, SIDE):
                remote(ref, ref, self.ts.at[j, off], self.tr.at[j, off], other).wait_recv()
            half = self.t.at[j, place()[3]]
            remote(half, half, self.hs.at[j], self.hr.at[j], other).start()

    def multiply(self, j, other, stage, dense):
        half = self.t.at[j, 1 - place()[3]]
        remote(half, half, self.hs.at[j], self.hr.at[j], other).wait_recv()
        stage[...] = self.w[j].reshape(stage.shape)
        rank = jnp.int32(0)
        for n in range(NB * NB):
            r, q = n // NB, n % NB
            keep = self.flags[j, 0, self.lane + n]
            tile = stage[jnp.minimum(rank, CAP - 1)]
            dense[r * BLK : (r + 1) * BLK, q * BLK : (q + 1) * BLK] = tile * keep.astype(F32).astype(BF16)
            rank = rank + keep
        _, _, lines, rows, width = self.t.shape
        left, right = self.t[j, 0].reshape(lines * rows, width), self.t[j, 1].reshape(lines * rows, width)
        self.acc[...] += (
            jnp.dot(left, dense[:width], preferred_element_type=F32)
            + jnp.dot(right, dense[width:], preferred_element_type=F32)
        ).reshape(self.acc.shape)

    def sum_copy(self, n):
        a, rows = self.a, self.acc.shape[1] // 2
        right, left, far = wrap(a + 1, SIDE), wrap(a - 1, SIDE), wrap(a + 2, SIDE)
        top, low = pl.ds(0, rows), pl.ds(rows, rows)
        src, dst, to = (
            (self.acc.at[far, top], self.far_in.at[0], right),
            (self.acc.at[far, low], self.far_in.at[1], left),
            (self.acc.at[right, low], self.near_in.at[0], right),
            (self.acc.at[left, top], self.near_in.at[1], left),
            (self.acc.at[right, top], self.near_in.at[2], right),
            (self.acc.at[left, low], self.near_in.at[3], left),
        )[n]
        return remote(src, dst, self.rs.at[n], self.rr.at[n], self.dev(to))

    def sum_start(self):
        for n in range(4):
            self.sum_copy(n).start()

    def sum_relay(self):
        a, rows = self.a, self.acc.shape[1] // 2
        self.sum_copy(0).wait_recv()
        self.acc[wrap(a + 1, SIDE), :rows] += self.far_in[0]
        self.sum_copy(4).start()
        self.sum_copy(1).wait_recv()
        self.acc[wrap(a - 1, SIDE), rows:] += self.far_in[1]
        self.sum_copy(5).start()

    def total(self):
        rows = self.acc.shape[1] // 2
        for n in range(2, 6):
            self.sum_copy(n).wait_recv()
        top = self.acc[self.a, :rows] + self.near_in[1] + self.near_in[2]
        low = self.acc[self.a, rows:] + self.near_in[0] + self.near_in[3]
        return top, low

    def drain(self, other):
        for j in range(SIDE):
            ref = self.block(j)
            for off in range(1, SIDE):
                remote(ref, ref, self.ts.at[j, off], self.tr.at[j, off], other).wait_send()
            half = self.t.at[j, place()[3]]
            remote(half, half, self.hs.at[j], self.hr.at[j], other).wait_send()
        for n in range(6):
            self.sum_copy(n).wait_send()
        self.weights.drain()
        self.masks.drain()


def hidden_kernel(m_in, g_in, u_in, t_in, d_in, hid, far_d, mg, mu, ring, stage, dense, *refs):
    x, y, z, c = place()
    zs, zr, ds, dr, ls = refs[-5:]
    per = len(refs[:-5]) // 2
    g_refs, u_refs = refs[:per], refs[per : 2 * per]
    gate = Product(True, (g_refs[0], mg) + g_refs[1:])
    up_ = Product(False, (u_refs[0], mu) + u_refs[1:])
    up, down = device(x, y, wrap(z + 1, RING), c), device(x, y, wrap(z - 1, RING), c)
    other = device(x, y, z, 1 - c)
    own = [
        pltpu.make_async_copy(src, dst, ls.at[i])
        for i, (src, dst) in enumerate(
            (
                (t_in, ring.at[z]),
                (g_in, gate.w.at[y]),
                (u_in, up_.w.at[x]),
                (m_in, gate.m.at[y]),
                (m_in, up_.m.at[x]),
            )
        )
    ]
    for cp in own:
        cp.start()
    greet(
        [device(wrap(x + k, SIDE), y, z, c) for k in (1, 2, 3)]
        + [device(x, wrap(y + k, SIDE), z, c) for k in (1, 2, 3)]
        + [up, down, other]
    )
    for cp in own:
        cp.wait()
    sends = []
    both = (gate, up_)

    def z_copy(block, dev, send, recv):
        return remote(ring.at[block], ring.at[block], send, recv, dev)

    def z_step(k):
        cp = z_copy(wrap(z - (k - 1), RING), up, zs.at[2 * k - 2], zr.at[2 * k - 2])
        cp.start()
        sends.append(cp)
        if k < RING // 2:
            cp = z_copy(wrap(z + (k - 1), RING), down, zs.at[2 * k - 1], zr.at[2 * k - 1])
            cp.start()
            sends.append(cp)

    def blocks(k):
        return (wrap(z - k, RING), wrap(z + k, RING))[: 1 if k in (0, RING // 2) else 2]

    def z_go(k):
        z_copy(wrap(z - k, RING), up, zs.at[2 * k - 2], zr.at[2 * k - 2]).wait_recv()
        if k < RING // 2:
            z_copy(wrap(z + k, RING), down, zs.at[2 * k - 1], zr.at[2 * k - 1]).wait_recv()
            z_step(k + 1)
        for s in blocks(k):
            for product in both:
                product.dispatch(ring.at[s], s)

    def z_collect(k):
        for s in blocks(k):
            for product in both:
                product.collect(s, other)

    z_step(1)
    for product in both:
        product.masks.first()
    for product in both:
        product.dispatch(ring.at[z], z)
    for product in both:
        product.weights.first()
    d_copy = remote(d_in, far_d, ds.at[0], dr.at[0], other)
    d_copy.start()
    for product in both:
        product.acc[...] = jnp.zeros_like(product.acc)
    z_go(1)
    for product in both:
        product.masks.relay()
    z_go(2)
    z_collect(0)
    z_go(3)
    z_collect(1)
    for product in both:
        product.weights.relay()
    for product in both:
        product.masks.far()
    flag_copies = [
        pltpu.make_async_copy(product.m, product.flags, ls.at[i]) for i, product in enumerate(both)
    ]
    for cp in flag_copies:
        cp.start()
    for k in range(4, RING // 2 + 1):
        z_go(k)
        z_collect(k - 2)
    for product in both:
        product.weights.far()
    z_collect(RING // 2 - 1)
    z_collect(RING // 2)
    for cp in flag_copies:
        cp.wait()

    for product in both:

        @pl.loop(0, SIDE)
        def _(n, product=product):
            j = wrap(lax.div(z, SIDE) + n, SIDE)
            product.multiply(j, other, stage, dense)

        if product is up_:
            gate.sum_relay()
        product.sum_start()
    up_.sum_relay()
    for n, (a, b) in enumerate(zip(gate.total(), up_.total())):
        hid[n] = (a / (1.0 + jnp.exp(-a)) * b).astype(BF16)
    remote(d_in, far_d, ds.at[0], dr.at[0], other).wait_recv()
    d_copy.wait_send()
    for product in both:
        product.drain(other)
    for cp in sends:
        cp.wait_send()


def make_hidden(m, g, u, t, d):
    dma = pltpu.SemaphoreType.DMA
    rows, width = t.shape
    product = [
        pltpu.VMEM((SIDE, PACK, BLK), BF16),
        pltpu.VMEM((SIDE, 2, SIDE, rows, width), BF16),
        pltpu.VMEM((SIDE, rows, SHARD), F32),
        pltpu.VMEM((2, rows // 2, SHARD), F32),
        pltpu.VMEM((4, rows // 2, SHARD), F32),
        pltpu.SMEM((SIDE,) + m.shape, jnp.int32),
        dma((4,)),
        dma((4,)),
        dma((4,)),
        dma((4,)),
        dma((SIDE, SIDE)),
        dma((SIDE, SIDE)),
        dma((SIDE,)),
        dma((SIDE,)),
        dma((SIDE,)),
        dma((6,)),
        dma((6,)),
    ]
    hid, far_d, _, _ = pl.pallas_call(
        hidden_kernel,
        out_shape=[
            jax.ShapeDtypeStruct((2, rows // 2, SHARD), BF16),
            jax.ShapeDtypeStruct(d.shape, BF16),
            jax.ShapeDtypeStruct((SIDE,) + m.shape, m.dtype),
            jax.ShapeDtypeStruct((SIDE,) + m.shape, m.dtype),
        ],
        in_specs=[pl.BlockSpec(memory_space=HBM)] * 5,
        out_specs=[
            pl.BlockSpec(memory_space=VMEM),
            pl.BlockSpec(memory_space=HBM),
            pl.BlockSpec(memory_space=HBM),
            pl.BlockSpec(memory_space=HBM),
        ],
        scratch_shapes=[
            pltpu.VMEM((RING, rows, width), BF16),
            pltpu.VMEM((CAP, BLK, BLK), BF16),
            pltpu.VMEM((SHARD, SHARD), BF16),
        ]
        + product * 2
        + [dma((15,))] * 2
        + [dma((1,))] * 2
        + [dma((5,))],
        compiler_params=pltpu.CompilerParams(collective_id=0, has_side_effects=True, vmem_limit_bytes=48 << 20),
        name="make_hidden",
    )(m, g, u, t, d)
    return hid, far_d


PARTS = 1
CHAINS = 4
LAG = 2
EARLY = 0


def tail_kernel(
    hid, d_own, d_far, o_ref, ha, hb, p, up_in, up_out, down_in, down_out, up_in16, up_out16, down_in16, down_out16,
    gs, gr, ps, pr, us, ur, ds, dr, ls,
):
    x, y, z, c = place()
    up, down = device(x, y, wrap(z + 1, RING), c), device(x, y, wrap(z - 1, RING), c)
    other = device(x, y, z, 1 - c)
    me = y * SIDE + x
    piece = ha.shape[2]
    bit = piece // CHAINS
    own = [
        pltpu.make_async_copy(hid.at[c, pl.ds(q * piece, piece)], ha.at[q, me], ls.at[q]) for q in range(PARTS)
    ]
    for cp in own:
        cp.start()
    greet(
        (
            device(wrap(x + 1, SIDE), y, z, c),
            device(wrap(x - 1, SIDE), y, z, c),
            device(x, wrap(y + 1, SIDE), z, c),
            device(x, wrap(y - 1, SIDE), z, c),
            up,
            down,
            other,
        )
    )
    swaps = [
        remote(hid.at[1 - c, pl.ds(q * piece, piece)], hb.at[q, me], ps.at[q], pr.at[q], other) for q in range(PARTS)
    ]
    for cp in swaps:
        cp.start()
    for cp in own:
        cp.wait()
    a = [Gather(ha.at[q], piece, True, gs.at[q], gr.at[q]) for q in range(PARTS)]
    b = [Gather(hb.at[q], piece, False, gs.at[PARTS + q], gr.at[PARTS + q]) for q in range(PARTS)]
    sends = []
    far_up, far_down = RING // 2, RING // 2 - 1

    def begin(q):
        a[q].first()
        a[q].second(0)
        swaps[q].wait_recv()
        b[q].first()
        b[q].second(0)

    def near(q):
        for s in (a[q], b[q]):
            s.relay()
            s.second(1)
            s.second(2)

    def middle(q):
        for s in (a[q], b[q]):
            s.relay2(0)
        for s in (a[q], b[q]):
            s.far()
            s.second(3)

    def late(q):
        for i in (1, 2, 3):
            for s in (a[q], b[q]):
                s.relay2(i)

    def ways(q, r):
        n = q * CHAINS + r
        return (
            (up_in, up_out, up_in16, up_out16, up, us.at[n], ur.at[n], far_up, 1),
            (down_in, down_out, down_in16, down_out16, down, ds.at[n], dr.at[n], far_down, -1),
        )

    def hop(k, n, way):
        wide_in, wide_out, thin_in, thin_out, dev, ss, rs, _, _ = way
        if k < EARLY:
            return thin_out.at[k, n], remote(thin_out.at[k, n], thin_in.at[k, n], ss.at[k], rs.at[k], dev)
        return wide_out.at[k - EARLY, n], remote(wide_out.at[k - EARLY, n], wide_in.at[k - EARLY, n], ss.at[k], rs.at[k], dev)

    def arrived(k, n, way):
        hop(k, n, way)[1].wait_recv()
        return way[2][k, n].astype(F32) if k < EARLY else way[0][k - EARLY, n]

    def mine(q, r, block):
        return p[q, block, r * bit : (r + 1) * bit]

    def end(q):
        for i in range(4):
            for s in (a[q], b[q]):
                s.far2(i)

    def multiply(q):
        blocks, _, width = ha.shape[1:]
        left = ha[q].reshape(blocks * piece, width)
        right = hb[q].reshape(blocks * piece, width)
        sums = jnp.dot(left, d_own[...], preferred_element_type=F32) + jnp.dot(
            right, d_far[...], preferred_element_type=F32
        )
        p[q] = sums.reshape(p.shape[1:])
        for r in range(CHAINS):
            n = q * CHAINS + r
            for way in ways(q, r):
                ref, cp = hop(0, n, way)
                ref[...] = mine(q, r, wrap(z + way[-1] * way[-2], RING)).astype(ref.dtype)
                cp.start()
                sends.append(cp)

    def step(k, q):
        for r in range(CHAINS):
            n = q * CHAINS + r
            for way in ways(q, r):
                far, sign = way[-2], way[-1]
                if k < far:
                    total = arrived(k - 1, n, way) + mine(q, r, wrap(z + sign * (far - k), RING))
                    ref, cp = hop(k, n, way)
                    ref[...] = total.astype(ref.dtype)
                    cp.start()
                    sends.append(cp)
            if k == far_up:
                total = mine(q, r, z)
                for way in ways(q, r):
                    total = total + arrived(way[-2] - 1, n, way)
                row = q * piece + r * bit
                o_ref[row : row + bit, :] = total.astype(BF16)

    stages = (begin, near, middle, late, end, multiply)
    at = [0] * PARTS
    for tick in range(LAG * (PARTS - 1) + len(stages)):
        for q in range(PARTS):
            if at[q] and at[q] <= far_up:
                step(at[q], q)
                at[q] += 1
        for q in range(PARTS):
            n = tick - LAG * q
            if 0 <= n < len(stages):
                stages[n](q)
                at[q] = int(n == len(stages) - 1)
    while min(at) <= far_up:
        for q in range(PARTS):
            if at[q] <= far_up:
                step(at[q], q)
                at[q] += 1
    for cp in swaps:
        cp.wait_send()
    for s in a + b:
        s.drain()
    for cp in sends:
        cp.wait_send()


def tail(hid, d_own, d_far):
    dma = pltpu.SemaphoreType.DMA
    _, rows, width = hid.shape
    cols = d_own.shape[1]
    chips = SIDE * SIDE
    n_up, n_down = RING // 2, RING // 2 - 1
    piece = rows // PARTS
    chains = PARTS * CHAINS
    bit = piece // CHAINS
    return pl.pallas_call(
        tail_kernel,
        out_shape=jax.ShapeDtypeStruct((rows, cols), BF16),
        in_specs=[pl.BlockSpec(memory_space=HBM)] + [pl.BlockSpec(memory_space=VMEM)] * 2,
        out_specs=pl.BlockSpec(memory_space=VMEM),
        scratch_shapes=[
            pltpu.VMEM((PARTS, chips, piece, width), BF16),
            pltpu.VMEM((PARTS, chips, piece, width), BF16),
            pltpu.VMEM((PARTS, chips, piece, cols), F32),
        ]
        + [pltpu.VMEM((max(n - EARLY, 1), chains, bit, cols), F32) for n in (n_up, n_up, n_down, n_down)]
        + [pltpu.VMEM((max(EARLY, 1), chains, bit, cols), BF16) for _ in range(4)]
        + [dma((2 * PARTS, 20))] * 2
        + [dma((PARTS,))] * 2
        + [dma((chains, n_up))] * 2
        + [dma((chains, n_down))] * 2
        + [dma((PARTS,))],
        compiler_params=pltpu.CompilerParams(collective_id=1, has_side_effects=True, vmem_limit_bytes=48 << 20),
        name="tail",
    )(hid, d_own, d_far)


def local(tokens, gate_weight, up_weight, down_weight, gate_keep, up_keep, down_keep):
    m, g, u, d = pack(gate_weight, up_weight, down_weight, gate_keep, up_keep, down_keep)
    hid, far_d = make_hidden(m, g, u, tokens, d)
    return tail(hid, d, far_d)


def solution(mesh):
    return jax.shard_map(
        local,
        mesh=mesh,
        in_specs=(
            P("tok", "hid"),
            P("tok", "hid"),
            P("tok", "hid"),
            P("hid", "tok"),
            P("tok", "hid"),
            P("tok", "hid"),
            P("hid", "tok"),
        ),
        out_specs=P("hid", "tok"),
        check_vma=False,
    )
```

```python
import functools

import jax
import jax.numpy as jnp
from jax import lax
from jax.experimental import pallas as pl
from jax.experimental.pallas import tpu as pltpu
from jax.sharding import PartitionSpec as P

MESH = pl.DeviceIdType.MESH
HBM = pltpu.MemorySpace.HBM
VMEM = pltpu.MemorySpace.VMEM
INPUTS = HBM
BF16 = jnp.bfloat16
F32 = jnp.float32

SIDE = 4
RING = 16
BLK = 128
NB = 4
CAP = 8
SHARD = NB * BLK
PACK = CAP * BLK
PIECES = 4


def place():
    t = lax.axis_index("tok")
    h = lax.axis_index("hid")
    return lax.rem(t, SIDE), lax.div(t, SIDE), lax.div(h, 2), lax.rem(h, 2)


def wrap(i, n):
    return lax.rem(i + n, n)


def device(x, y, z, c):
    return (y * SIDE + x, z * 2 + c)


def greet(peers):
    barrier = pltpu.get_barrier_semaphore()
    for peer in peers:
        pl.semaphore_signal(barrier, inc=1, device_id=peer, device_id_type=MESH)
    pl.semaphore_wait(barrier, len(peers))


class Gather:
    def __init__(self, buf, rows, x_first, send, recv):
        x, y, z, c = place()
        self.buf, self.send, self.recv = buf, send, recv
        self.split = rows > 1
        self.pieces = (pl.ds(0, rows // 2), pl.ds(rows // 2, rows // 2))
        self.a, self.b = (x, y) if x_first else (y, x)
        self.slot = lambda a, b: (b * SIDE + a) if x_first else (a * SIDE + b)
        self.dev = lambda a, b: device(a, b, z, c) if x_first else device(b, a, z, c)
        self.copies = {}

    def part(self, slot, piece):
        ref = self.buf.at[slot]
        if piece is None:
            return ref
        return ref.at[self.pieces[piece]]

    def copy(self, key, index, slot, piece, dev):
        ref = self.part(slot, piece)
        cp = pltpu.make_async_remote_copy(
            src_ref=ref,
            dst_ref=ref,
            send_sem=self.send.at[index],
            recv_sem=self.recv.at[index],
            device_id=dev,
            device_id_type=MESH,
        )
        cp.start()
        self.copies[key] = cp

    def got(self, index, slot, piece):
        ref = self.part(slot, piece)
        x, y, z, c = place()
        pltpu.make_async_remote_copy(
            src_ref=ref,
            dst_ref=ref,
            send_sem=self.send.at[index],
            recv_sem=self.recv.at[index],
            device_id=self.dev(wrap(self.a + 1, SIDE), self.b),
            device_id_type=MESH,
        ).wait_recv()

    def first(self):
        s = self.slot(self.a, self.b)
        self.copy("r", 0, s, None, self.dev(wrap(self.a + 1, SIDE), self.b))
        self.copy("l", 1, s, None, self.dev(wrap(self.a - 1, SIDE), self.b))

    def relay(self):
        left = self.slot(wrap(self.a - 1, SIDE), self.b)
        right = self.slot(wrap(self.a + 1, SIDE), self.b)
        self.got(0, left, None)
        self.copy("fr", 2, left, 0 if self.split else None, self.dev(wrap(self.a + 1, SIDE), self.b))
        self.got(1, right, None)
        if self.split:
            self.copy("fl", 3, right, 1, self.dev(wrap(self.a - 1, SIDE), self.b))

    def far(self):
        opposite = self.slot(wrap(self.a + 2, SIDE), self.b)
        self.got(2, opposite, 0 if self.split else None)
        if self.split:
            self.got(3, opposite, 1)

    OFF = (0, -1, 1, 2)

    def second(self, i):
        a = wrap(self.a + self.OFF[i], SIDE)
        s = self.slot(a, self.b)
        self.copy(("u", i), 4 + 4 * i, s, None, self.dev(self.a, wrap(self.b + 1, SIDE)))
        self.copy(("d", i), 5 + 4 * i, s, None, self.dev(self.a, wrap(self.b - 1, SIDE)))

    def relay2(self, i):
        a = wrap(self.a + self.OFF[i], SIDE)
        below = self.slot(a, wrap(self.b - 1, SIDE))
        above = self.slot(a, wrap(self.b + 1, SIDE))
        self.got(4 + 4 * i, below, None)
        self.copy(("fu", i), 6 + 4 * i, below, 0 if self.split else None, self.dev(self.a, wrap(self.b + 1, SIDE)))
        self.got(5 + 4 * i, above, None)
        if self.split:
            self.copy(("fd", i), 7 + 4 * i, above, 1, self.dev(self.a, wrap(self.b - 1, SIDE)))

    def far2(self, i):
        a = wrap(self.a + self.OFF[i], SIDE)
        s = self.slot(a, wrap(self.b + 2, SIDE))
        self.got(6 + 4 * i, s, 0 if self.split else None)
        if self.split:
            self.got(7 + 4 * i, s, 1)

    def drain(self):
        for cp in self.copies.values():
            cp.wait_send()


def pack_kernel(gk_ref, uk_ref, dk_ref, gw_in, uw_in, dw_in, m_ref, g_ref, u_ref, d_ref, gw_ref, uw_ref, dw_ref, sem):
    loads = [
        pltpu.make_async_copy(src, dst, sem.at[i])
        for i, (src, dst) in enumerate(((gw_in, gw_ref), (uw_in, uw_ref), (dw_in, dw_ref)))
    ]
    for cp in loads:
        cp.start()
    lane = lax.broadcasted_iota(jnp.int32, m_ref.shape, 1)
    flags = jnp.zeros(m_ref.shape, jnp.int32)
    for m, (keep_ref, w_ref, o_ref) in enumerate(((gk_ref, gw_ref, g_ref), (uk_ref, uw_ref, u_ref))):
        o_ref[...] = jnp.zeros_like(o_ref)
        loads[m].wait()
        rank = jnp.int32(0)
        for b in range(NB * NB):
            i, j = b // NB, b % NB
            keep = keep_ref[i, j]

            @pl.when(keep == 1)
            def _(i=i, j=j, rank=rank, w_ref=w_ref, o_ref=o_ref):
                row = pl.multiple_of(jnp.minimum(rank, CAP - 1) * BLK, BLK)
                o_ref[pl.ds(row, BLK), :] = w_ref[i * BLK : (i + 1) * BLK, j * BLK : (j + 1) * BLK]

            flags = jnp.where(lane == m * NB * NB + b, keep, flags)
            rank = rank + keep
    m_ref[...] = flags
    loads[2].wait()
    for i in range(NB):
        for j in range(NB):
            r, s = slice(i * BLK, (i + 1) * BLK), slice(j * BLK, (j + 1) * BLK)
            d_ref[r, s] = dw_ref[r, s] * dk_ref[i, j].astype(F32).astype(BF16)


def pack(gw, uw, dw, gk, uk, dk):
    return pl.pallas_call(
        pack_kernel,
        in_specs=[pl.BlockSpec(memory_space=pltpu.MemorySpace.SMEM)] * 3 + [pl.BlockSpec(memory_space=HBM)] * 3,
        scratch_shapes=[pltpu.VMEM(w.shape, w.dtype) for w in (gw, uw, dw)] + [pltpu.SemaphoreType.DMA((3,))],
        out_specs=[pl.BlockSpec(memory_space=VMEM)] * 4,
        out_shape=[
            jax.ShapeDtypeStruct((1, BLK), jnp.int32),
            jax.ShapeDtypeStruct((PACK, BLK), BF16),
            jax.ShapeDtypeStruct((PACK, BLK), BF16),
            jax.ShapeDtypeStruct(dw.shape, BF16),
        ],
        name="pack",
    )(gk, uk, dk, gw, uw, dw)


def remote(src, dst, send, recv, dev):
    return pltpu.make_async_remote_copy(
        src_ref=src, dst_ref=dst, send_sem=send, recv_sem=recv, device_id=dev, device_id_type=MESH
    )


class Line(Gather):
    def __init__(self, buf, rows, along_x, send, recv):
        super().__init__(buf, rows, along_x, send, recv)
        self.slot = lambda a, b: a


class Product:
    def __init__(self, split_x, refs):
        x, y, z, c = place()
        self.a, self.b = (x, y) if split_x else (y, x)
        self.dev = lambda a: device(a, y, z, c) if split_x else device(x, a, z, c)
        self.part = (lambda s: (lax.rem(s, SIDE), lax.div(s, SIDE))) if split_x else (
            lambda s: (lax.div(s, SIDE), lax.rem(s, SIDE))
        )
        (self.w, self.m, self.t, self.acc, self.far_in, self.near_in, self.flags) = refs[:7]
        ws, wr, ms, mr, self.ts, self.tr, self.tl, self.hs, self.hr, self.rs, self.rr = refs[7:]
        self.lane = 0 if split_x else NB * NB
        self.weights = Line(self.w, PACK, not split_x, ws, wr)
        self.masks = Line(self.m, 1, not split_x, ms, mr)

    def block(self, j):
        return self.t.at[j, place()[3], self.a]

    def dispatch(self, src, s):
        to, j = self.part(s)
        off = wrap(to - self.a, SIDE)

        @pl.when(off == 0)
        def _():
            pltpu.make_async_copy(src, self.block(j), self.tl.at[j]).start()

        @pl.when(off != 0)
        def _():
            remote(src, self.block(j), self.ts.at[j, off], self.tr.at[j, off], self.dev(to)).start()

    def collect(self, s, other):
        to, j = self.part(s)

        @pl.when(to == self.a)
        def _():
            ref = self.block(j)
            pltpu.make_async_copy(ref, ref, self.tl.at[j]).wait()
            for off in range(1, SIDE):
                remote(ref, ref, self.ts.at[j, off], self.tr.at[j, off], other).wait_recv()
            half = self.t.at[j, place()[3]]
            remote(half, half, self.hs.at[j], self.hr.at[j], other).start()

    def multiply(self, j, other, stage, dense):
        half = self.t.at[j, 1 - place()[3]]
        remote(half, half, self.hs.at[j], self.hr.at[j], other).wait_recv()
        stage[...] = self.w[j].reshape(stage.shape)
        rank = jnp.int32(0)
        for n in range(NB * NB):
            r, q = n // NB, n % NB
            keep = self.flags[j, 0, self.lane + n]
            tile = stage[jnp.minimum(rank, CAP - 1)]
            dense[r * BLK : (r + 1) * BLK, q * BLK : (q + 1) * BLK] = tile * keep.astype(F32).astype(BF16)
            rank = rank + keep
        _, _, lines, rows, width = self.t.shape
        left, right = self.t[j, 0].reshape(lines * rows, width), self.t[j, 1].reshape(lines * rows, width)
        self.acc[...] += (
            jnp.dot(left, dense[:width], preferred_element_type=F32)
            + jnp.dot(right, dense[width:], preferred_element_type=F32)
        ).reshape(self.acc.shape)

    def sum_copy(self, n):
        a, rows = self.a, self.acc.shape[1] // 2
        right, left, far = wrap(a + 1, SIDE), wrap(a - 1, SIDE), wrap(a + 2, SIDE)
        top, low = pl.ds(0, rows), pl.ds(rows, rows)
        src, dst, to = (
            (self.acc.at[far, top], self.far_in.at[0], right),
            (self.acc.at[far, low], self.far_in.at[1], left),
            (self.acc.at[right, low], self.near_in.at[0], right),
            (self.acc.at[left, top], self.near_in.at[1], left),
            (self.acc.at[right, top], self.near_in.at[2], right),
            (self.acc.at[left, low], self.near_in.at[3], left),
        )[n]
        return remote(src, dst, self.rs.at[n], self.rr.at[n], self.dev(to))

    def sum_start(self):
        for n in range(4):
            self.sum_copy(n).start()

    def sum_relay(self):
        a, rows = self.a, self.acc.shape[1] // 2
        self.sum_copy(0).wait_recv()
        self.acc[wrap(a + 1, SIDE), :rows] += self.far_in[0]
        self.sum_copy(4).start()
        self.sum_copy(1).wait_recv()
        self.acc[wrap(a - 1, SIDE), rows:] += self.far_in[1]
        self.sum_copy(5).start()

    def total(self):
        rows = self.acc.shape[1] // 2
        for n in range(2, 6):
            self.sum_copy(n).wait_recv()
        top = self.acc[self.a, :rows] + self.near_in[1] + self.near_in[2]
        low = self.acc[self.a, rows:] + self.near_in[0] + self.near_in[3]
        return top, low

    def drain(self, other):
        for j in range(SIDE):
            ref = self.block(j)
            for off in range(1, SIDE):
                remote(ref, ref, self.ts.at[j, off], self.tr.at[j, off], other).wait_send()
            half = self.t.at[j, place()[3]]
            remote(half, half, self.hs.at[j], self.hr.at[j], other).wait_send()
        for n in range(6):
            self.sum_copy(n).wait_send()
        self.weights.drain()
        self.masks.drain()


def hidden_phase(m_in, g_in, u_in, t_in, d_in, mg, mu, hid, d_own, d_far, ring, stage, dense, *refs):
    x, y, z, c = place()
    zs, zr, ds, dr, ls = refs[-5:]
    per = len(refs[:-5]) // 2
    g_refs, u_refs = refs[:per], refs[per : 2 * per]
    gate = Product(True, (g_refs[0], mg) + g_refs[1:])
    up_ = Product(False, (u_refs[0], mu) + u_refs[1:])
    up, down = device(x, y, wrap(z + 1, RING), c), device(x, y, wrap(z - 1, RING), c)
    other = device(x, y, z, 1 - c)
    own = [
        pltpu.make_async_copy(src, dst, ls.at[i])
        for i, (src, dst) in enumerate(
            (
                (t_in, ring.at[z]),
                (g_in, gate.w.at[y]),
                (u_in, up_.w.at[x]),
                (m_in, gate.m.at[y]),
                (m_in, up_.m.at[x]),
                (d_in, d_own),
            )
        )
    ]
    for cp in own:
        cp.start()
    greet(
        [device(wrap(x + k, SIDE), y, z, c) for k in (1, 2, 3)]
        + [device(x, wrap(y + k, SIDE), z, c) for k in (1, 2, 3)]
        + [up, down, other]
    )
    for cp in own:
        cp.wait()
    sends = []
    both = (gate, up_)

    size = t_in.shape[0] // PIECES

    def z_copy(k, p, sign, block):
        ref = ring.at[block, pl.ds(p * size, size)]
        n = 2 * k - 2 if sign > 0 else 2 * k - 1
        return remote(ref, ref, zs.at[n, p], zr.at[n, p], up if sign > 0 else down)

    def z_step(k, p):
        for sign in (1, -1) if k < RING // 2 else (1,):
            cp = z_copy(k, p, sign, wrap(z - sign * (k - 1), RING))
            cp.start()
            sends.append(cp)

    def blocks(k):
        return (wrap(z - k, RING), wrap(z + k, RING))[: 1 if k in (0, RING // 2) else 2]

    def z_go(k):
        for p in range(PIECES):
            for sign in (1, -1) if k < RING // 2 else (1,):
                z_copy(k, p, sign, wrap(z - sign * k, RING)).wait_recv()
            if k < RING // 2:
                z_step(k + 1, p)
        for s in blocks(k):
            for product in both:
                product.dispatch(ring.at[s], s)

    def z_collect(k):
        for s in blocks(k):
            for product in both:
                product.collect(s, other)

    for p in range(PIECES):
        z_step(1, p)
    for product in both:
        product.masks.first()
    for product in both:
        product.dispatch(ring.at[z], z)
    for product in both:
        product.weights.first()
    d_copy = remote(d_in, d_far, ds.at[0], dr.at[0], other)
    d_copy.start()
    for product in both:
        product.acc[...] = jnp.zeros_like(product.acc)
    z_go(1)
    for product in both:
        product.masks.relay()
    z_go(2)
    z_collect(0)
    z_go(3)
    z_collect(1)
    for product in both:
        product.weights.relay()
    for product in both:
        product.masks.far()
    flag_copies = [
        pltpu.make_async_copy(product.m, product.flags, ls.at[i]) for i, product in enumerate(both)
    ]
    for cp in flag_copies:
        cp.start()
    for k in range(4, RING // 2 + 1):
        z_go(k)
        z_collect(k - 2)
    for product in both:
        product.weights.far()
    z_collect(RING // 2 - 1)
    z_collect(RING // 2)
    for cp in flag_copies:
        cp.wait()

    for product in both:

        @pl.loop(0, SIDE)
        def _(n, product=product):
            j = wrap(lax.div(z, SIDE) + n, SIDE)
            product.multiply(j, other, stage, dense)

        if product is up_:
            gate.sum_relay()
        product.sum_start()
    up_.sum_relay()
    for n, (a, b) in enumerate(zip(gate.total(), up_.total())):
        hid[n] = (a / (1.0 + jnp.exp(-a)) * b).astype(BF16)
    d_copy.wait_recv()
    d_copy.wait_send()
    for product in both:
        product.drain(other)
    for cp in sends:
        cp.wait_send()


PARTS = 1
CHAINS = 4
LAG = 2
EARLY = 0


def tail_phase(
    hid, d_own, d_far, o_ref, ha, hb, p, up_in, up_out, down_in, down_out, up_in16, up_out16, down_in16, down_out16,
    gs, gr, ps, pr, us, ur, ds, dr, ls,
):
    x, y, z, c = place()
    up, down = device(x, y, wrap(z + 1, RING), c), device(x, y, wrap(z - 1, RING), c)
    other = device(x, y, z, 1 - c)
    me = y * SIDE + x
    piece = ha.shape[2]
    bit = piece // CHAINS
    own = [
        pltpu.make_async_copy(hid.at[c, pl.ds(q * piece, piece)], ha.at[q, me], ls.at[q]) for q in range(PARTS)
    ]
    for cp in own:
        cp.start()
    swaps = [
        remote(hid.at[1 - c, pl.ds(q * piece, piece)], hb.at[q, me], ps.at[q], pr.at[q], other) for q in range(PARTS)
    ]
    for cp in swaps:
        cp.start()
    for cp in own:
        cp.wait()
    a = [Gather(ha.at[q], piece, True, gs.at[q], gr.at[q]) for q in range(PARTS)]
    b = [Gather(hb.at[q], piece, False, gs.at[PARTS + q], gr.at[PARTS + q]) for q in range(PARTS)]
    sends = []
    far_up, far_down = RING // 2, RING // 2 - 1

    def begin(q):
        a[q].first()
        a[q].second(0)
        swaps[q].wait_recv()
        b[q].first()
        b[q].second(0)

    def near(q):
        for s in (a[q], b[q]):
            s.relay()
            s.second(1)
            s.second(2)

    def middle(q):
        for s in (a[q], b[q]):
            s.relay2(0)
        for s in (a[q], b[q]):
            s.far()
            s.second(3)

    def late(q):
        for i in (1, 2, 3):
            for s in (a[q], b[q]):
                s.relay2(i)

    def ways(q, r):
        n = q * CHAINS + r
        return (
            (up_in, up_out, up_in16, up_out16, up, us.at[n], ur.at[n], far_up, 1),
            (down_in, down_out, down_in16, down_out16, down, ds.at[n], dr.at[n], far_down, -1),
        )

    def hop(k, n, way):
        wide_in, wide_out, thin_in, thin_out, dev, ss, rs, _, _ = way
        if k < EARLY:
            return thin_out.at[k, n], remote(thin_out.at[k, n], thin_in.at[k, n], ss.at[k], rs.at[k], dev)
        return wide_out.at[k - EARLY, n], remote(wide_out.at[k - EARLY, n], wide_in.at[k - EARLY, n], ss.at[k], rs.at[k], dev)

    def arrived(k, n, way):
        hop(k, n, way)[1].wait_recv()
        return way[2][k, n].astype(F32) if k < EARLY else way[0][k - EARLY, n]

    def mine(q, r, block):
        return p[q, block, r * bit : (r + 1) * bit]

    def end(q):
        for i in range(4):
            for s in (a[q], b[q]):
                s.far2(i)

    def multiply(q):
        blocks, _, width = ha.shape[1:]
        left = ha[q].reshape(blocks * piece, width)
        right = hb[q].reshape(blocks * piece, width)
        sums = jnp.dot(left, d_own[...], preferred_element_type=F32) + jnp.dot(
            right, d_far[...], preferred_element_type=F32
        )
        p[q] = sums.reshape(p.shape[1:])
        for r in range(CHAINS):
            n = q * CHAINS + r
            for way in ways(q, r):
                ref, cp = hop(0, n, way)
                ref[...] = mine(q, r, wrap(z + way[-1] * way[-2], RING)).astype(ref.dtype)
                cp.start()
                sends.append(cp)

    def step(k, q):
        for r in range(CHAINS):
            n = q * CHAINS + r
            for way in ways(q, r):
                far, sign = way[-2], way[-1]
                if k < far:
                    total = arrived(k - 1, n, way) + mine(q, r, wrap(z + sign * (far - k), RING))
                    ref, cp = hop(k, n, way)
                    ref[...] = total.astype(ref.dtype)
                    cp.start()
                    sends.append(cp)
            if k == far_up:
                total = mine(q, r, z)
                for way in ways(q, r):
                    total = total + arrived(way[-2] - 1, n, way)
                row = q * piece + r * bit
                o_ref[row : row + bit, :] = total.astype(BF16)

    stages = (begin, near, middle, late, end, multiply)
    at = [0] * PARTS
    for tick in range(LAG * (PARTS - 1) + len(stages)):
        for q in range(PARTS):
            if at[q] and at[q] <= far_up:
                step(at[q], q)
                at[q] += 1
        for q in range(PARTS):
            n = tick - LAG * q
            if 0 <= n < len(stages):
                stages[n](q)
                at[q] = int(n == len(stages) - 1)
    while min(at) <= far_up:
        for q in range(PARTS):
            if at[q] <= far_up:
                step(at[q], q)
                at[q] += 1
    for cp in swaps:
        cp.wait_send()
    for s in a + b:
        s.drain()
    for cp in sends:
        cp.wait_send()


def layer_kernel(*refs):
    ins, o_ref, masks = refs[:5], refs[5], refs[6:8]
    kept, first, last = refs[8:11], refs[11 : 11 + N_FIRST], refs[11 + N_FIRST :]
    hidden_phase(*ins, *masks, *kept, *first)
    tail_phase(*kept, o_ref, *last)


N_FIRST = 3 + 2 * 17 + 5


def layer(m, g, u, t, d):
    dma = pltpu.SemaphoreType.DMA
    rows, width = t.shape
    cols = d.shape[1]
    chips = SIDE * SIDE
    n_up, n_down = RING // 2, RING // 2 - 1
    half = rows // 2
    piece = half // PARTS
    chains = PARTS * CHAINS
    bit = piece // CHAINS
    product = [
        pltpu.VMEM((SIDE, PACK, BLK), BF16),
        pltpu.VMEM((SIDE, 2, SIDE, rows, width), BF16),
        pltpu.VMEM((SIDE, rows, SHARD), F32),
        pltpu.VMEM((2, half, SHARD), F32),
        pltpu.VMEM((4, half, SHARD), F32),
        pltpu.SMEM((SIDE,) + m.shape, jnp.int32),
        dma((4,)),
        dma((4,)),
        dma((4,)),
        dma((4,)),
        dma((SIDE, SIDE)),
        dma((SIDE, SIDE)),
        dma((SIDE,)),
        dma((SIDE,)),
        dma((SIDE,)),
        dma((6,)),
        dma((6,)),
    ]
    kept = [pltpu.VMEM((2, half, SHARD), BF16), pltpu.VMEM(d.shape, BF16), pltpu.VMEM(d.shape, BF16)]
    first = (
        [
            pltpu.VMEM((RING, rows, width), BF16),
            pltpu.VMEM((CAP, BLK, BLK), BF16),
            pltpu.VMEM((SHARD, SHARD), BF16),
        ]
        + product * 2
        + [dma((RING - 1, PIECES))] * 2
        + [dma((1,))] * 2
        + [dma((6,))]
    )
    assert len(first) == N_FIRST
    last = (
        [
            pltpu.VMEM((PARTS, chips, piece, SHARD), BF16),
            pltpu.VMEM((PARTS, chips, piece, SHARD), BF16),
            pltpu.VMEM((PARTS, chips, piece, cols), F32),
        ]
        + [pltpu.VMEM((max(n - EARLY, 1), chains, bit, cols), F32) for n in (n_up, n_up, n_down, n_down)]
        + [pltpu.VMEM((max(EARLY, 1), chains, bit, cols), BF16) for _ in range(4)]
        + [dma((2 * PARTS, 20))] * 2
        + [dma((PARTS,))] * 2
        + [dma((chains, n_up))] * 2
        + [dma((chains, n_down))] * 2
        + [dma((PARTS,))]
    )
    out, _, _ = pl.pallas_call(
        layer_kernel,
        out_shape=[
            jax.ShapeDtypeStruct((half, cols), BF16),
            jax.ShapeDtypeStruct((SIDE,) + m.shape, m.dtype),
            jax.ShapeDtypeStruct((SIDE,) + m.shape, m.dtype),
        ],
        in_specs=[pl.BlockSpec(memory_space=INPUTS)] * 5,
        out_specs=[
            pl.BlockSpec(memory_space=VMEM),
            pl.BlockSpec(memory_space=HBM),
            pl.BlockSpec(memory_space=HBM),
        ],
        scratch_shapes=kept + first + last,
        compiler_params=pltpu.CompilerParams(collective_id=0, has_side_effects=True, vmem_limit_bytes=48 << 20),
        name="layer",
    )(m, g, u, t, d)
    return out


def local(tokens, gate_weight, up_weight, down_weight, gate_keep, up_keep, down_keep):
    m, g, u, d = pack(gate_weight, up_weight, down_weight, gate_keep, up_keep, down_keep)
    return layer(m, g, u, tokens, d)


def solution(mesh):
    return jax.shard_map(
        local,
        mesh=mesh,
        in_specs=(
            P("tok", "hid"),
            P("tok", "hid"),
            P("tok", "hid"),
            P("hid", "tok"),
            P("tok", "hid"),
            P("tok", "hid"),
            P("hid", "tok"),
        ),
        out_specs=P("hid", "tok"),
        check_vma=False,
    )
```

```python
import functools

import jax
import jax.numpy as jnp
from jax import lax
from jax.experimental import pallas as pl
from jax.experimental.pallas import tpu as pltpu
from jax.sharding import PartitionSpec as P

MESH = pl.DeviceIdType.MESH
HBM = pltpu.MemorySpace.HBM
VMEM = pltpu.MemorySpace.VMEM
INPUTS = HBM
BF16 = jnp.bfloat16
F32 = jnp.float32

SIDE = 4
RING = 16
BLK = 128
NB = 4
CAP = 8
SHARD = NB * BLK
PACK = CAP * BLK


def place():
    t = lax.axis_index("tok")
    h = lax.axis_index("hid")
    return lax.rem(t, SIDE), lax.div(t, SIDE), lax.div(h, 2), lax.rem(h, 2)


def wrap(i, n):
    return lax.rem(i + n, n)


def device(x, y, z, c):
    return (y * SIDE + x, z * 2 + c)


def greet(peers):
    barrier = pltpu.get_barrier_semaphore()
    for peer in peers:
        pl.semaphore_signal(barrier, inc=1, device_id=peer, device_id_type=MESH)
    pl.semaphore_wait(barrier, len(peers))


class Gather:
    def __init__(self, buf, rows, x_first, send, recv):
        x, y, z, c = place()
        self.buf, self.send, self.recv = buf, send, recv
        self.split = rows > 1
        self.pieces = (pl.ds(0, rows // 2), pl.ds(rows // 2, rows // 2))
        self.a, self.b = (x, y) if x_first else (y, x)
        self.slot = lambda a, b: (b * SIDE + a) if x_first else (a * SIDE + b)
        self.dev = lambda a, b: device(a, b, z, c) if x_first else device(b, a, z, c)
        self.copies = {}

    def part(self, slot, piece):
        ref = self.buf.at[slot]
        if piece is None:
            return ref
        return ref.at[self.pieces[piece]]

    def copy(self, key, index, slot, piece, dev):
        ref = self.part(slot, piece)
        cp = pltpu.make_async_remote_copy(
            src_ref=ref,
            dst_ref=ref,
            send_sem=self.send.at[index],
            recv_sem=self.recv.at[index],
            device_id=dev,
            device_id_type=MESH,
        )
        cp.start()
        self.copies[key] = cp

    def got(self, index, slot, piece):
        ref = self.part(slot, piece)
        x, y, z, c = place()
        pltpu.make_async_remote_copy(
            src_ref=ref,
            dst_ref=ref,
            send_sem=self.send.at[index],
            recv_sem=self.recv.at[index],
            device_id=self.dev(wrap(self.a + 1, SIDE), self.b),
            device_id_type=MESH,
        ).wait_recv()

    def first(self):
        s = self.slot(self.a, self.b)
        self.copy("r", 0, s, None, self.dev(wrap(self.a + 1, SIDE), self.b))
        self.copy("l", 1, s, None, self.dev(wrap(self.a - 1, SIDE), self.b))

    def relay(self):
        left = self.slot(wrap(self.a - 1, SIDE), self.b)
        right = self.slot(wrap(self.a + 1, SIDE), self.b)
        self.got(0, left, None)
        self.copy("fr", 2, left, 0 if self.split else None, self.dev(wrap(self.a + 1, SIDE), self.b))
        self.got(1, right, None)
        if self.split:
            self.copy("fl", 3, right, 1, self.dev(wrap(self.a - 1, SIDE), self.b))

    def far(self):
        opposite = self.slot(wrap(self.a + 2, SIDE), self.b)
        self.got(2, opposite, 0 if self.split else None)
        if self.split:
            self.got(3, opposite, 1)

    OFF = (0, -1, 1, 2)

    def second(self, i):
        a = wrap(self.a + self.OFF[i], SIDE)
        s = self.slot(a, self.b)
        self.copy(("u", i), 4 + 4 * i, s, None, self.dev(self.a, wrap(self.b + 1, SIDE)))
        self.copy(("d", i), 5 + 4 * i, s, None, self.dev(self.a, wrap(self.b - 1, SIDE)))

    def relay2(self, i):
        a = wrap(self.a + self.OFF[i], SIDE)
        below = self.slot(a, wrap(self.b - 1, SIDE))
        above = self.slot(a, wrap(self.b + 1, SIDE))
        self.got(4 + 4 * i, below, None)
        self.copy(("fu", i), 6 + 4 * i, below, 0 if self.split else None, self.dev(self.a, wrap(self.b + 1, SIDE)))
        self.got(5 + 4 * i, above, None)
        if self.split:
            self.copy(("fd", i), 7 + 4 * i, above, 1, self.dev(self.a, wrap(self.b - 1, SIDE)))

    def far2(self, i):
        a = wrap(self.a + self.OFF[i], SIDE)
        s = self.slot(a, wrap(self.b + 2, SIDE))
        self.got(6 + 4 * i, s, 0 if self.split else None)
        if self.split:
            self.got(7 + 4 * i, s, 1)

    def drain(self):
        for cp in self.copies.values():
            cp.wait_send()


def pack_kernel(gk_ref, uk_ref, dk_ref, gw_in, uw_in, dw_in, m_ref, g_ref, u_ref, d_ref, gw_ref, uw_ref, dw_ref, sem):
    loads = [
        pltpu.make_async_copy(src, dst, sem.at[i])
        for i, (src, dst) in enumerate(((gw_in, gw_ref), (uw_in, uw_ref), (dw_in, dw_ref)))
    ]
    for cp in loads:
        cp.start()
    lane = lax.broadcasted_iota(jnp.int32, m_ref.shape, 1)
    flags = jnp.zeros(m_ref.shape, jnp.int32)
    for m, (keep_ref, w_ref, o_ref) in enumerate(((gk_ref, gw_ref, g_ref), (uk_ref, uw_ref, u_ref))):
        o_ref[...] = jnp.zeros_like(o_ref)
        loads[m].wait()
        rank = jnp.int32(0)
        for b in range(NB * NB):
            i, j = b // NB, b % NB
            keep = keep_ref[i, j]

            @pl.when(keep == 1)
            def _(i=i, j=j, rank=rank, w_ref=w_ref, o_ref=o_ref):
                row = pl.multiple_of(jnp.minimum(rank, CAP - 1) * BLK, BLK)
                o_ref[pl.ds(row, BLK), :] = w_ref[i * BLK : (i + 1) * BLK, j * BLK : (j + 1) * BLK]

            flags = jnp.where(lane == m * NB * NB + b, keep, flags)
            rank = rank + keep
    m_ref[...] = flags
    loads[2].wait()
    for i in range(NB):
        for j in range(NB):
            r, s = slice(i * BLK, (i + 1) * BLK), slice(j * BLK, (j + 1) * BLK)
            d_ref[r, s] = dw_ref[r, s] * dk_ref[i, j].astype(F32).astype(BF16)


def pack(gw, uw, dw, gk, uk, dk):
    return pl.pallas_call(
        pack_kernel,
        in_specs=[pl.BlockSpec(memory_space=pltpu.MemorySpace.SMEM)] * 3 + [pl.BlockSpec(memory_space=HBM)] * 3,
        scratch_shapes=[pltpu.VMEM(w.shape, w.dtype) for w in (gw, uw, dw)] + [pltpu.SemaphoreType.DMA((3,))],
        out_specs=[pl.BlockSpec(memory_space=VMEM)] * 4,
        out_shape=[
            jax.ShapeDtypeStruct((1, BLK), jnp.int32),
            jax.ShapeDtypeStruct((PACK, BLK), BF16),
            jax.ShapeDtypeStruct((PACK, BLK), BF16),
            jax.ShapeDtypeStruct(dw.shape, BF16),
        ],
        name="pack",
    )(gk, uk, dk, gw, uw, dw)


def remote(src, dst, send, recv, dev):
    return pltpu.make_async_remote_copy(
        src_ref=src, dst_ref=dst, send_sem=send, recv_sem=recv, device_id=dev, device_id_type=MESH
    )


class Line(Gather):
    def __init__(self, buf, rows, along_x, send, recv):
        super().__init__(buf, rows, along_x, send, recv)
        self.slot = lambda a, b: a


class Product:
    def __init__(self, split_x, refs):
        x, y, z, c = place()
        self.a, self.b = (x, y) if split_x else (y, x)
        self.dev = lambda a: device(a, y, z, c) if split_x else device(x, a, z, c)
        self.part = (lambda s: (lax.rem(s, SIDE), lax.div(s, SIDE))) if split_x else (
            lambda s: (lax.div(s, SIDE), lax.rem(s, SIDE))
        )
        (self.w, self.m, self.t, self.acc, self.far_in, self.near_in, self.flags) = refs[:7]
        ws, wr, ms, mr, self.ts, self.tr, self.tl, self.hs, self.hr, self.rs, self.rr = refs[7:]
        self.lane = 0 if split_x else NB * NB
        self.weights = Line(self.w, PACK, not split_x, ws, wr)
        self.masks = Line(self.m, 1, not split_x, ms, mr)

    def block(self, j):
        return self.t.at[j, place()[3], self.a]

    def dispatch(self, src, s):
        to, j = self.part(s)
        off = wrap(to - self.a, SIDE)

        @pl.when(off == 0)
        def _():
            pltpu.make_async_copy(src, self.block(j), self.tl.at[j]).start()

        @pl.when(off != 0)
        def _():
            remote(src, self.block(j), self.ts.at[j, off], self.tr.at[j, off], self.dev(to)).start()

    def collect(self, s, other):
        to, j = self.part(s)

        @pl.when(to == self.a)
        def _():
            ref = self.block(j)
            pltpu.make_async_copy(ref, ref, self.tl.at[j]).wait()
            for off in range(1, SIDE):
                remote(ref, ref, self.ts.at[j, off], self.tr.at[j, off], other).wait_recv()
            half = self.t.at[j, place()[3]]
            remote(half, half, self.hs.at[j], self.hr.at[j], other).start()

    def multiply(self, j, other, stage, dense):
        half = self.t.at[j, 1 - place()[3]]
        remote(half, half, self.hs.at[j], self.hr.at[j], other).wait_recv()
        stage[...] = self.w[j].reshape(stage.shape)
        rank = jnp.int32(0)
        for n in range(NB * NB):
            r, q = n // NB, n % NB
            keep = self.flags[j, 0, self.lane + n]
            tile = stage[jnp.minimum(rank, CAP - 1)]
            dense[r * BLK : (r + 1) * BLK, q * BLK : (q + 1) * BLK] = tile * keep.astype(F32).astype(BF16)
            rank = rank + keep
        _, _, lines, rows, width = self.t.shape
        left, right = self.t[j, 0].reshape(lines * rows, width), self.t[j, 1].reshape(lines * rows, width)
        self.acc[...] += (
            jnp.dot(left, dense[:width], preferred_element_type=F32)
            + jnp.dot(right, dense[width:], preferred_element_type=F32)
        ).reshape(self.acc.shape)

    def sum_copy(self, n):
        a, rows = self.a, self.acc.shape[1] // 2
        right, left, far = wrap(a + 1, SIDE), wrap(a - 1, SIDE), wrap(a + 2, SIDE)
        top, low = pl.ds(0, rows), pl.ds(rows, rows)
        src, dst, to = (
            (self.acc.at[far, top], self.far_in.at[0], right),
            (self.acc.at[far, low], self.far_in.at[1], left),
            (self.acc.at[right, low], self.near_in.at[0], right),
            (self.acc.at[left, top], self.near_in.at[1], left),
            (self.acc.at[right, top], self.near_in.at[2], right),
            (self.acc.at[left, low], self.near_in.at[3], left),
        )[n]
        return remote(src, dst, self.rs.at[n], self.rr.at[n], self.dev(to))

    def sum_start(self):
        for n in range(4):
            self.sum_copy(n).start()

    def sum_relay(self):
        a, rows = self.a, self.acc.shape[1] // 2
        self.sum_copy(0).wait_recv()
        self.acc[wrap(a + 1, SIDE), :rows] += self.far_in[0]
        self.sum_copy(4).start()
        self.sum_copy(1).wait_recv()
        self.acc[wrap(a - 1, SIDE), rows:] += self.far_in[1]
        self.sum_copy(5).start()

    def total(self):
        rows = self.acc.shape[1] // 2
        for n in range(2, 6):
            self.sum_copy(n).wait_recv()
        top = self.acc[self.a, :rows] + self.near_in[1] + self.near_in[2]
        low = self.acc[self.a, rows:] + self.near_in[0] + self.near_in[3]
        return top, low

    def drain(self, other):
        for j in range(SIDE):
            ref = self.block(j)
            for off in range(1, SIDE):
                remote(ref, ref, self.ts.at[j, off], self.tr.at[j, off], other).wait_send()
            half = self.t.at[j, place()[3]]
            remote(half, half, self.hs.at[j], self.hr.at[j], other).wait_send()
        for n in range(6):
            self.sum_copy(n).wait_send()
        self.weights.drain()
        self.masks.drain()


def hidden_phase(m_in, g_in, u_in, t_in, d_in, mg, mu, hid, d_own, d_far, ring, stage, dense, *refs):
    x, y, z, c = place()
    zs, zr, ds, dr, ls = refs[-5:]
    per = len(refs[:-5]) // 2
    g_refs, u_refs = refs[:per], refs[per : 2 * per]
    gate = Product(True, (g_refs[0], mg) + g_refs[1:])
    up_ = Product(False, (u_refs[0], mu) + u_refs[1:])
    other = device(x, y, z, 1 - c)
    own = [
        pltpu.make_async_copy(src, dst, ls.at[i])
        for i, (src, dst) in enumerate(
            (
                (t_in, ring.at[z]),
                (g_in, gate.w.at[y]),
                (u_in, up_.w.at[x]),
                (m_in, gate.m.at[y]),
                (m_in, up_.m.at[x]),
                (d_in, d_own),
            )
        )
    ]
    for cp in own:
        cp.start()
    greet(
        [device(wrap(x + k, SIDE), y, z, c) for k in (1, 2, 3)]
        + [device(x, wrap(y + k, SIDE), z, c) for k in (1, 2, 3)]
        + [device(x, y, wrap(z + k, RING), c) for k in (1, 2, -1, -2)]
        + [other]
    )
    for cp in own:
        cp.wait()
    sends = []
    both = (gate, up_)

    def z_copy(d, have):
        ref = ring.at[wrap(z - have, RING)]
        n = 2 * d - 2 if d > 0 else -2 * d - 1
        return remote(ref, ref, zs.at[n], zr.at[n], device(x, y, wrap(z + d - have, RING), c))

    def z_send(d, have):
        cp = z_copy(d, have)
        cp.start()
        sends.append(cp)

    def z_wait(d):
        z_copy(d, d - (1 if d > 0 else -1)).wait_recv()

    def dispatch(*ds):
        for d in ds:
            for product in both:
                product.dispatch(ring.at[wrap(z - d, RING)], wrap(z - d, RING))

    def collect(*ds):
        for d in ds:
            for product in both:
                product.collect(wrap(z - d, RING), other)

    def z_go(far):
        for sign in (1, -1):
            d = sign * far
            z_wait(d)
            if far + 2 <= (RING // 2 if sign > 0 else RING // 2 - 1):
                z_send(d + 2 * sign, d)
            z_send(d + sign, d)
        dispatch(far, -far)
        for sign in (1, -1):
            z_wait(sign * (far - 1))
        dispatch(far - 1, 1 - far)

    for d in (2, -2, 1, -1):
        z_send(d, 0)
    for product in both:
        product.masks.first()
    dispatch(0)
    for product in both:
        product.weights.first()
    d_copy = remote(d_in, d_far, ds.at[0], dr.at[0], other)
    d_copy.start()
    for product in both:
        product.acc[...] = jnp.zeros_like(product.acc)
    z_go(2)
    for product in both:
        product.masks.relay()
    collect(0)
    z_go(4)
    for product in both:
        product.weights.relay()
    collect(2, -2, 1, -1)
    for product in both:
        product.masks.far()
    flag_copies = [
        pltpu.make_async_copy(product.m, product.flags, ls.at[i]) for i, product in enumerate(both)
    ]
    for cp in flag_copies:
        cp.start()
    z_go(6)
    collect(4, -4, 3, -3)
    z_wait(8)
    dispatch(8)
    for d in (7, -7):
        z_wait(d)
    dispatch(7, -7)
    for product in both:
        product.weights.far()
    collect(6, -6, 5, -5, 8, 7, -7)
    for cp in flag_copies:
        cp.wait()

    for product in both:

        @pl.loop(0, SIDE)
        def _(n, product=product):
            j = wrap(lax.div(z, SIDE) + n, SIDE)
            product.multiply(j, other, stage, dense)

        if product is up_:
            gate.sum_relay()
        product.sum_start()
    up_.sum_relay()
    for n, (a, b) in enumerate(zip(gate.total(), up_.total())):
        hid[n] = (a / (1.0 + jnp.exp(-a)) * b).astype(BF16)
    d_copy.wait_recv()
    d_copy.wait_send()
    for product in both:
        product.drain(other)
    for cp in sends:
        cp.wait_send()


CHAINS = 2


def tail_phase(hid, d_own, d_far, o_ref, ha, hb, p, up_out, up_far, up_near, down_out, down_far, down_near,
    as_, ar, bs, br, ps, pr, ufs, ufr, uns, unr, dfs, dfr, dns, dnr, ls,
):
    x, y, z, c = place()
    other = device(x, y, z, 1 - c)
    me = y * SIDE + x
    rows = ha.shape[1]
    bit = rows // CHAINS
    own = pltpu.make_async_copy(hid.at[c], ha.at[me], ls.at[0])
    own.start()
    swap = remote(hid.at[1 - c], hb.at[me], ps.at[0], pr.at[0], other)
    swap.start()
    own.wait()
    a = Gather(ha, rows, True, as_, ar)
    b = Gather(hb, rows, False, bs, br)
    a.first()
    a.second(0)
    swap.wait_recv()
    b.first()
    b.second(0)
    for s in (a, b):
        s.relay()
        s.second(1)
        s.second(2)
    for s in (a, b):
        s.relay2(0)
    for s in (a, b):
        s.far()
        s.second(3)
    for i in (1, 2, 3):
        for s in (a, b):
            s.relay2(i)
    for i in range(4):
        for s in (a, b):
            s.far2(i)
    blocks, _, width = ha.shape
    sums = jnp.dot(ha[...].reshape(blocks * rows, width), d_own[...], preferred_element_type=F32) + jnp.dot(
        hb[...].reshape(blocks * rows, width), d_far[...], preferred_element_type=F32
    )
    p[...] = sums.reshape(p.shape)

    ways = (
        (1, RING // 2, up_out, up_far, up_near, ufs, ufr, uns, unr),
        (-1, RING // 2 - 1, down_out, down_far, down_near, dfs, dfr, dns, dnr),
    )
    sends = []

    def mine(sign, k, r):
        return p[wrap(z + sign * k, RING), r * bit : (r + 1) * bit]

    def hop(way, k, r):
        sign, _, out, far, near, fs, fr, ns, nr = way
        stop, step = (k - 2) // 2 if k % 2 == 0 else (k - 1) // 2, 2 - k % 2
        dst, ss, rs = (near, ns, nr) if k % 2 else (far, fs, fr)
        to = device(x, y, wrap(z + sign * step, RING), c)
        return remote(out.at[k, r], dst.at[stop, r], ss.at[stop, r], rs.at[stop, r], to)

    def push(way, k, r, value):
        way[2][k, r] = value.astype(BF16)
        cp = hop(way, k, r)
        cp.start()
        sends.append(cp)

    def take(way, k, r, value):
        far, near = way[3], way[4]
        hop(way, k + 1, r).wait_recv()
        value = value + near[k // 2, r].astype(F32)
        if k + 2 <= way[1]:
            hop(way, k + 2, r).wait_recv()
            value = value + far[k // 2, r].astype(F32)
        return value

    for k in (8, 7, 5, 3, 1):
        for r in range(CHAINS):
            for way in ways:
                if k <= way[1]:
                    push(way, k, r, mine(way[0], k, r))
    for k in (6, 4, 2):
        for r in range(CHAINS):
            for way in ways:
                push(way, k, r, take(way, k, r, mine(way[0], k, r)))
    for r in range(CHAINS):
        total = mine(1, 0, r)
        for way in ways:
            total = take(way, 0, r, total)
        o_ref[r * bit : (r + 1) * bit, :] = total.astype(BF16)
    swap.wait_send()
    a.drain()
    b.drain()
    for cp in sends:
        cp.wait_send()


def layer_kernel(*refs):
    ins, o_ref, masks = refs[:5], refs[5], refs[6:8]
    kept, first, last = refs[8:11], refs[11 : 11 + N_FIRST], refs[11 + N_FIRST :]
    hidden_phase(*ins, *masks, *kept, *first)
    tail_phase(*kept, o_ref, *last)


N_FIRST = 3 + 2 * 17 + 5


def layer(m, g, u, t, d):
    dma = pltpu.SemaphoreType.DMA
    rows, width = t.shape
    cols = d.shape[1]
    chips = SIDE * SIDE
    half = rows // 2
    bit = half // CHAINS
    stops = RING // 4
    product = [
        pltpu.VMEM((SIDE, PACK, BLK), BF16),
        pltpu.VMEM((SIDE, 2, SIDE, rows, width), BF16),
        pltpu.VMEM((SIDE, rows, SHARD), F32),
        pltpu.VMEM((2, half, SHARD), F32),
        pltpu.VMEM((4, half, SHARD), F32),
        pltpu.SMEM((SIDE,) + m.shape, jnp.int32),
        dma((4,)),
        dma((4,)),
        dma((4,)),
        dma((4,)),
        dma((SIDE, SIDE)),
        dma((SIDE, SIDE)),
        dma((SIDE,)),
        dma((SIDE,)),
        dma((SIDE,)),
        dma((6,)),
        dma((6,)),
    ]
    kept = [pltpu.VMEM((2, half, SHARD), BF16), pltpu.VMEM(d.shape, BF16), pltpu.VMEM(d.shape, BF16)]
    first = (
        [
            pltpu.VMEM((RING, rows, width), BF16),
            pltpu.VMEM((CAP, BLK, BLK), BF16),
            pltpu.VMEM((SHARD, SHARD), BF16),
        ]
        + product * 2
        + [dma((RING - 1,))] * 2
        + [dma((1,))] * 2
        + [dma((6,))]
    )
    assert len(first) == N_FIRST
    last = (
        [
            pltpu.VMEM((chips, half, SHARD), BF16),
            pltpu.VMEM((chips, half, SHARD), BF16),
            pltpu.VMEM((chips, half, cols), F32),
        ]
        + [pltpu.VMEM((n, CHAINS, bit, cols), BF16) for n in (RING // 2 + 1, stops, stops)] * 2
        + [dma((20,))] * 4
        + [dma((1,))] * 2
        + [dma((stops, CHAINS))] * 8
        + [dma((1,))]
    )
    out, _, _ = pl.pallas_call(
        layer_kernel,
        out_shape=[
            jax.ShapeDtypeStruct((half, cols), BF16),
            jax.ShapeDtypeStruct((SIDE,) + m.shape, m.dtype),
            jax.ShapeDtypeStruct((SIDE,) + m.shape, m.dtype),
        ],
        in_specs=[pl.BlockSpec(memory_space=INPUTS)] * 5,
        out_specs=[
            pl.BlockSpec(memory_space=VMEM),
            pl.BlockSpec(memory_space=HBM),
            pl.BlockSpec(memory_space=HBM),
        ],
        scratch_shapes=kept + first + last,
        compiler_params=pltpu.CompilerParams(collective_id=0, has_side_effects=True),
        name="layer",
    )(m, g, u, t, d)
    return out


def local(tokens, gate_weight, up_weight, down_weight, gate_keep, up_keep, down_keep):
    m, g, u, d = pack(gate_weight, up_weight, down_weight, gate_keep, up_keep, down_keep)
    return layer(m, g, u, tokens, d)


def solution(mesh):
    return jax.shard_map(
        local,
        mesh=mesh,
        in_specs=(
            P("tok", "hid"),
            P("tok", "hid"),
            P("tok", "hid"),
            P("hid", "tok"),
            P("tok", "hid"),
            P("tok", "hid"),
            P("hid", "tok"),
        ),
        out_specs=P("hid", "tok"),
        check_vma=False,
    )
```

```python
import functools

import jax
import jax.numpy as jnp
from jax import lax
from jax.experimental import pallas as pl
from jax.experimental.pallas import tpu as pltpu
from jax.sharding import PartitionSpec as P

MESH = pl.DeviceIdType.MESH
HBM = pltpu.MemorySpace.HBM
VMEM = pltpu.MemorySpace.VMEM
INPUTS = HBM
BF16 = jnp.bfloat16
F32 = jnp.float32

SIDE = 4
RING = 16
BLK = 128
NB = 4
CAP = 8
SHARD = NB * BLK
PACK = CAP * BLK


def place():
    t = lax.axis_index("tok")
    h = lax.axis_index("hid")
    return lax.rem(t, SIDE), lax.div(t, SIDE), lax.div(h, 2), lax.rem(h, 2)


def wrap(i, n):
    return lax.rem(i + n, n)


def device(x, y, z, c):
    return (y * SIDE + x, z * 2 + c)


def greet(peers):
    barrier = pltpu.get_barrier_semaphore()
    for peer in peers:
        pl.semaphore_signal(barrier, inc=1, device_id=peer, device_id_type=MESH)
    pl.semaphore_wait(barrier, len(peers))


class Gather:
    relayed = False

    def __init__(self, buf, rows, x_first, send, recv):
        x, y, z, c = place()
        self.buf, self.send, self.recv = buf, send, recv
        self.pieces = (pl.ds(0, rows // 2), pl.ds(rows // 2, rows // 2))
        self.a, self.b = (x, y) if x_first else (y, x)
        self.slot = lambda a, b: (b * SIDE + a) if x_first else (a * SIDE + b)
        self.dev = lambda a, b: device(a, b, z, c) if x_first else device(b, a, z, c)
        self.copies = {}

    def part(self, slot, piece):
        ref = self.buf.at[slot]
        if piece is None:
            return ref
        return ref.at[self.pieces[piece]]

    def copy(self, key, index, slot, piece, dev):
        ref = self.part(slot, piece)
        cp = pltpu.make_async_remote_copy(
            src_ref=ref,
            dst_ref=ref,
            send_sem=self.send.at[index],
            recv_sem=self.recv.at[index],
            device_id=dev,
            device_id_type=MESH,
        )
        cp.start()
        self.copies[key] = cp

    def got(self, index, slot, piece):
        ref = self.part(slot, piece)
        x, y, z, c = place()
        pltpu.make_async_remote_copy(
            src_ref=ref,
            dst_ref=ref,
            send_sem=self.send.at[index],
            recv_sem=self.recv.at[index],
            device_id=self.dev(wrap(self.a + 1, SIDE), self.b),
            device_id_type=MESH,
        ).wait_recv()

    def first(self):
        s = self.slot(self.a, self.b)
        self.copy("r", 0, s, None, self.dev(wrap(self.a + 1, SIDE), self.b))
        self.copy("l", 1, s, None, self.dev(wrap(self.a - 1, SIDE), self.b))
        if not self.relayed:
            self.copy("f", 2, s, None, self.dev(wrap(self.a + 2, SIDE), self.b))

    def relay(self):
        left = self.slot(wrap(self.a - 1, SIDE), self.b)
        right = self.slot(wrap(self.a + 1, SIDE), self.b)
        self.got(0, left, None)
        if self.relayed:
            self.copy("fr", 2, left, 0, self.dev(wrap(self.a + 1, SIDE), self.b))
        self.got(1, right, None)
        if self.relayed:
            self.copy("fl", 3, right, 1, self.dev(wrap(self.a - 1, SIDE), self.b))

    def far(self):
        opposite = self.slot(wrap(self.a + 2, SIDE), self.b)
        if self.relayed:
            self.got(2, opposite, 0)
            self.got(3, opposite, 1)
        else:
            self.got(2, opposite, None)

    OFF = (0, -1, 1, 2)

    def second(self, i):
        a = wrap(self.a + self.OFF[i], SIDE)
        s = self.slot(a, self.b)
        self.copy(("u", i), 4 + 4 * i, s, None, self.dev(self.a, wrap(self.b + 1, SIDE)))
        self.copy(("d", i), 5 + 4 * i, s, None, self.dev(self.a, wrap(self.b - 1, SIDE)))

    def relay2(self, i):
        a = wrap(self.a + self.OFF[i], SIDE)
        below = self.slot(a, wrap(self.b - 1, SIDE))
        above = self.slot(a, wrap(self.b + 1, SIDE))
        self.got(4 + 4 * i, below, None)
        self.copy(("fu", i), 6 + 4 * i, below, 0, self.dev(self.a, wrap(self.b + 1, SIDE)))
        self.got(5 + 4 * i, above, None)
        self.copy(("fd", i), 7 + 4 * i, above, 1, self.dev(self.a, wrap(self.b - 1, SIDE)))

    def far2(self, i):
        a = wrap(self.a + self.OFF[i], SIDE)
        s = self.slot(a, wrap(self.b + 2, SIDE))
        self.got(6 + 4 * i, s, 0)
        self.got(7 + 4 * i, s, 1)

    def drain(self):
        for cp in self.copies.values():
            cp.wait_send()


def pack_kernel(gk_ref, uk_ref, dk_ref, gw_in, uw_in, dw_in, m_ref, g_ref, u_ref, d_ref, gw_ref, uw_ref, dw_ref, sem):
    loads = [
        pltpu.make_async_copy(src, dst, sem.at[i])
        for i, (src, dst) in enumerate(((gw_in, gw_ref), (uw_in, uw_ref), (dw_in, dw_ref)))
    ]
    for cp in loads:
        cp.start()
    lane = lax.broadcasted_iota(jnp.int32, m_ref.shape, 1)
    flags = jnp.zeros(m_ref.shape, jnp.int32)
    for m, (keep_ref, w_ref, o_ref) in enumerate(((gk_ref, gw_ref, g_ref), (uk_ref, uw_ref, u_ref))):
        o_ref[...] = jnp.zeros_like(o_ref)
        loads[m].wait()
        rank = jnp.int32(0)
        for b in range(NB * NB):
            i, j = b // NB, b % NB
            keep = keep_ref[i, j]

            @pl.when(keep == 1)
            def _(i=i, j=j, rank=rank, w_ref=w_ref, o_ref=o_ref):
                row = pl.multiple_of(jnp.minimum(rank, CAP - 1) * BLK, BLK)
                o_ref[pl.ds(row, BLK), :] = w_ref[i * BLK : (i + 1) * BLK, j * BLK : (j + 1) * BLK]

            flags = jnp.where(lane == m * NB * NB + b, keep, flags)
            rank = rank + keep
    m_ref[...] = flags
    loads[2].wait()
    for i in range(NB):
        for j in range(NB):
            r, s = slice(i * BLK, (i + 1) * BLK), slice(j * BLK, (j + 1) * BLK)
            d_ref[r, s] = dw_ref[r, s] * dk_ref[i, j].astype(F32).astype(BF16)


def pack(gw, uw, dw, gk, uk, dk):
    return pl.pallas_call(
        pack_kernel,
        in_specs=[pl.BlockSpec(memory_space=pltpu.MemorySpace.SMEM)] * 3 + [pl.BlockSpec(memory_space=HBM)] * 3,
        scratch_shapes=[pltpu.VMEM(w.shape, w.dtype) for w in (gw, uw, dw)] + [pltpu.SemaphoreType.DMA((3,))],
        out_specs=[pl.BlockSpec(memory_space=VMEM)] * 4,
        out_shape=[
            jax.ShapeDtypeStruct((1, BLK), jnp.int32),
            jax.ShapeDtypeStruct((PACK, BLK), BF16),
            jax.ShapeDtypeStruct((PACK, BLK), BF16),
            jax.ShapeDtypeStruct(dw.shape, BF16),
        ],
        name="pack",
    )(gk, uk, dk, gw, uw, dw)


def remote(src, dst, send, recv, dev):
    return pltpu.make_async_remote_copy(
        src_ref=src, dst_ref=dst, send_sem=send, recv_sem=recv, device_id=dev, device_id_type=MESH
    )


class Line(Gather):
    def __init__(self, buf, rows, along_x, send, recv):
        super().__init__(buf, rows, along_x, send, recv)
        self.slot = lambda a, b: a
        self.relayed = rows > 1


class Product:
    def __init__(self, split_x, refs):
        x, y, z, c = place()
        self.a, self.b = (x, y) if split_x else (y, x)
        self.dev = lambda a: device(a, y, z, c) if split_x else device(x, a, z, c)
        self.part = (lambda s: (lax.rem(s, SIDE), lax.div(s, SIDE))) if split_x else (
            lambda s: (lax.div(s, SIDE), lax.rem(s, SIDE))
        )
        (self.w, self.m, self.t, self.acc, self.far_in, self.near_in, self.flags) = refs[:7]
        ws, wr, ms, mr, self.ts, self.tr, self.tl, self.hs, self.hr, self.rs, self.rr = refs[7:]
        self.lane = 0 if split_x else NB * NB
        self.weights = Line(self.w, PACK, not split_x, ws, wr)
        self.masks = Line(self.m, 1, not split_x, ms, mr)

    def block(self, j):
        return self.t.at[j, place()[3], self.a]

    def dispatch(self, src, s):
        to, j = self.part(s)
        off = wrap(to - self.a, SIDE)

        @pl.when(off == 0)
        def _():
            pltpu.make_async_copy(src, self.block(j), self.tl.at[j]).start()

        @pl.when(off != 0)
        def _():
            remote(src, self.block(j), self.ts.at[j, off], self.tr.at[j, off], self.dev(to)).start()

    def collect(self, s, other):
        to, j = self.part(s)

        @pl.when(to == self.a)
        def _():
            ref = self.block(j)
            pltpu.make_async_copy(ref, ref, self.tl.at[j]).wait()
            for off in range(1, SIDE):
                remote(ref, ref, self.ts.at[j, off], self.tr.at[j, off], other).wait_recv()
            half = self.t.at[j, place()[3]]
            remote(half, half, self.hs.at[j], self.hr.at[j], other).start()

    def multiply(self, j, p, stage, dense):
        stage[...] = self.w[j].reshape(stage.shape)
        half = NB // 2
        rank = jnp.int32(0)
        for n in range(half * NB):
            rank = rank + self.flags[j, 0, self.lane + n]
        rank = rank * p
        for n in range(half * NB):
            r, q = n // NB, n % NB
            keep = self.flags[j, 0, self.lane + p * half * NB + n]
            tile = stage[jnp.minimum(rank, CAP - 1)]
            dense[r * BLK : (r + 1) * BLK, q * BLK : (q + 1) * BLK] = tile * keep.astype(F32).astype(BF16)
            rank = rank + keep
        _, _, lines, rows, width = self.t.shape
        features = self.t[j, p].reshape(lines * rows, width)
        self.acc[...] += jnp.dot(features, dense[...], preferred_element_type=F32).reshape(self.acc.shape)

    def shared(self, j, other):
        half = self.t.at[j, 1 - place()[3]]
        remote(half, half, self.hs.at[j], self.hr.at[j], other).wait_recv()

    def sum_copy(self, n):
        a, rows = self.a, self.acc.shape[1] // 2
        right, left, far = wrap(a + 1, SIDE), wrap(a - 1, SIDE), wrap(a + 2, SIDE)
        top, low = pl.ds(0, rows), pl.ds(rows, rows)
        src, dst, to = (
            (self.acc.at[far, top], self.far_in.at[0], right),
            (self.acc.at[far, low], self.far_in.at[1], left),
            (self.acc.at[right, low], self.near_in.at[0], right),
            (self.acc.at[left, top], self.near_in.at[1], left),
            (self.acc.at[right, top], self.near_in.at[2], right),
            (self.acc.at[left, low], self.near_in.at[3], left),
        )[n]
        return remote(src, dst, self.rs.at[n], self.rr.at[n], self.dev(to))

    def sum_start(self):
        for n in range(4):
            self.sum_copy(n).start()

    def sum_relay(self):
        a, rows = self.a, self.acc.shape[1] // 2
        self.sum_copy(0).wait_recv()
        self.acc[wrap(a + 1, SIDE), :rows] += self.far_in[0]
        self.sum_copy(4).start()
        self.sum_copy(1).wait_recv()
        self.acc[wrap(a - 1, SIDE), rows:] += self.far_in[1]
        self.sum_copy(5).start()

    def total(self):
        rows = self.acc.shape[1] // 2
        for n in range(2, 6):
            self.sum_copy(n).wait_recv()
        top = self.acc[self.a, :rows] + self.near_in[1] + self.near_in[2]
        low = self.acc[self.a, rows:] + self.near_in[0] + self.near_in[3]
        return top, low

    def drain(self, other):
        for j in range(SIDE):
            ref = self.block(j)
            for off in range(1, SIDE):
                remote(ref, ref, self.ts.at[j, off], self.tr.at[j, off], other).wait_send()
            half = self.t.at[j, place()[3]]
            remote(half, half, self.hs.at[j], self.hr.at[j], other).wait_send()
        for n in range(6):
            self.sum_copy(n).wait_send()
        self.weights.drain()
        self.masks.drain()


def hidden_phase(m_in, g_in, u_in, t_in, d_in, mg, mu, hid, d_own, d_far, ring, stage, dense, *refs):
    x, y, z, c = place()
    zs, zr, ds, dr, ls = refs[-5:]
    per = len(refs[:-5]) // 2
    g_refs, u_refs = refs[:per], refs[per : 2 * per]
    gate = Product(True, (g_refs[0], mg) + g_refs[1:])
    up_ = Product(False, (u_refs[0], mu) + u_refs[1:])
    other = device(x, y, z, 1 - c)
    own = [
        pltpu.make_async_copy(src, dst, ls.at[i])
        for i, (src, dst) in enumerate(
            (
                (t_in, ring.at[z]),
                (g_in, gate.w.at[y]),
                (u_in, up_.w.at[x]),
                (m_in, gate.m.at[y]),
                (m_in, up_.m.at[x]),
                (d_in, d_own),
            )
        )
    ]
    for cp in own:
        cp.start()
    greet(
        [device(wrap(x + k, SIDE), y, z, c) for k in (1, 2, 3)]
        + [device(x, wrap(y + k, SIDE), z, c) for k in (1, 2, 3)]
        + [device(x, y, wrap(z + k, RING), c) for k in (1, 2, -1, -2)]
        + [other]
    )
    for cp in own:
        cp.wait()
    sends = []
    both = (gate, up_)

    def z_copy(d, have):
        ref = ring.at[wrap(z - have, RING)]
        n = 2 * d - 2 if d > 0 else -2 * d - 1
        return remote(ref, ref, zs.at[n], zr.at[n], device(x, y, wrap(z + d - have, RING), c))

    def z_send(d, have):
        cp = z_copy(d, have)
        cp.start()
        sends.append(cp)

    def z_wait(d):
        z_copy(d, d - (1 if d > 0 else -1)).wait_recv()

    def dispatch(*ds):
        for d in ds:
            for product in both:
                product.dispatch(ring.at[wrap(z - d, RING)], wrap(z - d, RING))

    def collect(*ds):
        for d in ds:
            for product in both:
                product.collect(wrap(z - d, RING), other)

    def z_go(far):
        for sign in (1, -1):
            d = sign * far
            z_wait(d)
            if far + 2 <= (RING // 2 if sign > 0 else RING // 2 - 1):
                z_send(d + 2 * sign, d)
            z_send(d + sign, d)
        dispatch(far, -far)
        for sign in (1, -1):
            z_wait(sign * (far - 1))
        dispatch(far - 1, 1 - far)

    for d in (2, -2, 1, -1):
        z_send(d, 0)
    for product in both:
        product.masks.first()
    dispatch(0)
    for product in both:
        product.weights.first()
    d_copy = remote(d_in, d_far, ds.at[0], dr.at[0], other)
    d_copy.start()
    for product in both:
        product.acc[...] = jnp.zeros_like(product.acc)
    z_go(2)
    for product in both:
        product.masks.relay()
    collect(0)
    z_go(4)
    for product in both:
        product.weights.relay()
    collect(2, -2, 1, -1)
    for product in both:
        product.masks.far()
    flag_copies = [
        pltpu.make_async_copy(product.m, product.flags, ls.at[i]) for i, product in enumerate(both)
    ]
    for cp in flag_copies:
        cp.start()
    z_go(6)
    collect(4, -4, 3, -3)
    z_wait(8)
    dispatch(8)
    for d in (7, -7):
        z_wait(d)
    dispatch(7, -7)
    for product in both:
        product.weights.far()
    collect(6, -6, 5, -5, 8, 7, -7)
    for cp in flag_copies:
        cp.wait()

    for product in both:

        @pl.loop(0, SIDE)
        def _(n, product=product):
            product.multiply(wrap(lax.div(z, SIDE) + n, SIDE), c, stage, dense)

    for product in both:

        @pl.loop(0, SIDE)
        def _(n, product=product):
            j = wrap(lax.div(z, SIDE) + n, SIDE)
            product.shared(j, other)
            product.multiply(j, 1 - c, stage, dense)

        if product is up_:
            gate.sum_relay()
        product.sum_start()
    up_.sum_relay()
    for n, (a, b) in enumerate(zip(gate.total(), up_.total())):
        hid[n] = (a / (1.0 + jnp.exp(-a)) * b).astype(BF16)
    d_copy.wait_recv()
    d_copy.wait_send()
    for product in both:
        product.drain(other)
    for cp in sends:
        cp.wait_send()


CHAINS = 2


def tail_phase(hid, d_own, d_far, o_ref, ha, hb, p, up_out, up_far, up_near, down_out, down_far, down_near,
    as_, ar, bs, br, ps, pr, ufs, ufr, uns, unr, dfs, dfr, dns, dnr, ls,
):
    x, y, z, c = place()
    other = device(x, y, z, 1 - c)
    me = y * SIDE + x
    rows = ha.shape[1]
    bit = rows // CHAINS
    own = pltpu.make_async_copy(hid.at[c], ha.at[me], ls.at[0])
    own.start()
    swap = remote(hid.at[1 - c], hb.at[me], ps.at[0], pr.at[0], other)
    swap.start()
    own.wait()
    a = Gather(ha, rows, True, as_, ar)
    b = Gather(hb, rows, False, bs, br)
    a.first()
    a.second(0)
    swap.wait_recv()
    b.first()
    b.second(0)
    for s in (a, b):
        s.relay()
        s.second(1)
        s.second(2)
    for s in (a, b):
        s.far()
        s.second(3)
    for i in range(4):
        for s in (a, b):
            s.relay2(i)
    for i in range(4):
        for s in (a, b):
            s.far2(i)
    blocks, _, width = ha.shape
    sums = jnp.dot(ha[...].reshape(blocks * rows, width), d_own[...], preferred_element_type=F32) + jnp.dot(
        hb[...].reshape(blocks * rows, width), d_far[...], preferred_element_type=F32
    )
    p[...] = sums.reshape(p.shape)

    ways = (
        (1, RING // 2, up_out, up_far, up_near, ufs, ufr, uns, unr),
        (-1, RING // 2 - 1, down_out, down_far, down_near, dfs, dfr, dns, dnr),
    )
    sends = []

    def mine(sign, k, r):
        return p[wrap(z + sign * k, RING), r * bit : (r + 1) * bit]

    def hop(way, k, r):
        sign, _, out, far, near, fs, fr, ns, nr = way
        stop, step = (k - 2) // 2 if k % 2 == 0 else (k - 1) // 2, 2 - k % 2
        dst, ss, rs = (near, ns, nr) if k % 2 else (far, fs, fr)
        to = device(x, y, wrap(z + sign * step, RING), c)
        return remote(out.at[k, r], dst.at[stop, r], ss.at[stop, r], rs.at[stop, r], to)

    def push(way, k, r, value):
        way[2][k, r] = value.astype(BF16)
        cp = hop(way, k, r)
        cp.start()
        sends.append(cp)

    def take(way, k, r, value):
        far, near = way[3], way[4]
        hop(way, k + 1, r).wait_recv()
        value = value + near[k // 2, r].astype(F32)
        if k + 2 <= way[1]:
            hop(way, k + 2, r).wait_recv()
            value = value + far[k // 2, r].astype(F32)
        return value

    for k in (8, 7, 5, 3, 1):
        for r in range(CHAINS):
            for way in ways:
                if k <= way[1]:
                    push(way, k, r, mine(way[0], k, r))
    for k in (6, 4, 2):
        for r in range(CHAINS):
            for way in ways:
                push(way, k, r, take(way, k, r, mine(way[0], k, r)))
    for r in range(CHAINS):
        total = mine(1, 0, r)
        for way in ways:
            total = take(way, 0, r, total)
        o_ref[r * bit : (r + 1) * bit, :] = total.astype(BF16)
    swap.wait_send()
    a.drain()
    b.drain()
    for cp in sends:
        cp.wait_send()


def layer_kernel(*refs):
    ins, o_ref, masks = refs[:5], refs[5], refs[6:8]
    kept, first, last = refs[8:11], refs[11 : 11 + N_FIRST], refs[11 + N_FIRST :]
    hidden_phase(*ins, *masks, *kept, *first)
    tail_phase(*kept, o_ref, *last)


N_FIRST = 3 + 2 * 17 + 5


def layer(m, g, u, t, d):
    dma = pltpu.SemaphoreType.DMA
    rows, width = t.shape
    cols = d.shape[1]
    chips = SIDE * SIDE
    half = rows // 2
    bit = half // CHAINS
    stops = RING // 4
    product = [
        pltpu.VMEM((SIDE, PACK, BLK), BF16),
        pltpu.VMEM((SIDE, 2, SIDE, rows, width), BF16),
        pltpu.VMEM((SIDE, rows, SHARD), F32),
        pltpu.VMEM((2, half, SHARD), F32),
        pltpu.VMEM((4, half, SHARD), F32),
        pltpu.SMEM((SIDE,) + m.shape, jnp.int32),
        dma((4,)),
        dma((4,)),
        dma((4,)),
        dma((4,)),
        dma((SIDE, SIDE)),
        dma((SIDE, SIDE)),
        dma((SIDE,)),
        dma((SIDE,)),
        dma((SIDE,)),
        dma((6,)),
        dma((6,)),
    ]
    kept = [pltpu.VMEM((2, half, SHARD), BF16), pltpu.VMEM(d.shape, BF16), pltpu.VMEM(d.shape, BF16)]
    first = (
        [
            pltpu.VMEM((RING, rows, width), BF16),
            pltpu.VMEM((CAP, BLK, BLK), BF16),
            pltpu.VMEM((SHARD // 2, SHARD), BF16),
        ]
        + product * 2
        + [dma((RING - 1,))] * 2
        + [dma((1,))] * 2
        + [dma((6,))]
    )
    assert len(first) == N_FIRST
    last = (
        [
            pltpu.VMEM((chips, half, SHARD), BF16),
            pltpu.VMEM((chips, half, SHARD), BF16),
            pltpu.VMEM((chips, half, cols), F32),
        ]
        + [pltpu.VMEM((n, CHAINS, bit, cols), BF16) for n in (RING // 2 + 1, stops, stops)] * 2
        + [dma((20,))] * 4
        + [dma((1,))] * 2
        + [dma((stops, CHAINS))] * 8
        + [dma((1,))]
    )
    out, _, _ = pl.pallas_call(
        layer_kernel,
        out_shape=[
            jax.ShapeDtypeStruct((half, cols), BF16),
            jax.ShapeDtypeStruct((SIDE,) + m.shape, m.dtype),
            jax.ShapeDtypeStruct((SIDE,) + m.shape, m.dtype),
        ],
        in_specs=[pl.BlockSpec(memory_space=INPUTS)] * 5,
        out_specs=[
            pl.BlockSpec(memory_space=VMEM),
            pl.BlockSpec(memory_space=HBM),
            pl.BlockSpec(memory_space=HBM),
        ],
        scratch_shapes=kept + first + last,
        compiler_params=pltpu.CompilerParams(collective_id=0, has_side_effects=True),
        name="layer",
    )(m, g, u, t, d)
    return out


def local(tokens, gate_weight, up_weight, down_weight, gate_keep, up_keep, down_keep):
    m, g, u, d = pack(gate_weight, up_weight, down_weight, gate_keep, up_keep, down_keep)
    return layer(m, g, u, tokens, d)


def solution(mesh):
    return jax.shard_map(
        local,
        mesh=mesh,
        in_specs=(
            P("tok", "hid"),
            P("tok", "hid"),
            P("tok", "hid"),
            P("hid", "tok"),
            P("tok", "hid"),
            P("tok", "hid"),
            P("hid", "tok"),
        ),
        out_specs=P("hid", "tok"),
        check_vma=False,
    )
```
